32 devices in a mesh: dom: 8 (over z, y), sub: 4 (over x, core).
Axes of the slice: x: 2, y: 2, z: 4, core: 2. Of those that a mesh axis runs over, the one named last changes fastest.
Arguments:
- displacement: float32 [3, 128, 64, 128], P(None, 'dom', 'sub'), may hold values from -0.3 to 0.3
- velocity: float32 [3, 128, 64, 128], P(None, 'dom', 'sub'), may hold values from -6 to 6
- modulus: float32 [128, 64, 128], P('dom', 'sub'), may hold values from 0.5 to 4
- element_stiffness: bfloat16 [24, 24], replicated, may hold values from -9 to 9.5, as said below
- viscosity: float32 [], replicated, may hold values from 0.1 to 0.4
- step_size: float32 [], replicated, may hold values from 0.3 to 0.6
- seg_tilt: float32 [2, 65536], P(None, ('dom', 'sub')), may hold values from -1.5 to 1.5
- seg_offset: float32 [65536], P(('dom', 'sub')), may hold values from -0.08 to 0.04
- seg_stiffness: float32 [65536], P(('dom', 'sub')), may hold values from 4 to 40
- projection: int32 [64, 128], P(('dom', 'sub')), may hold values from 0 to 65535, as said below
- contact_flag: int32 [64, 128], P(('dom', 'sub')), may hold values from 0 to 1
- candidates: int32 [64, 8], P(('dom', 'sub')), may hold values from -1 to 63, as said below
Outputs:
- new_velocity: float32 [3, 128, 64, 128], P(None, 'dom', 'sub')
- reaction: float32 [3, 65536], P(None, ('dom', 'sub'))
The draws below stay inside these ranges and needn't reach their ends.
Inputs may be any that keep to these rules, and one draw needn't show every extreme that they name: `element_stiffness`: symmetric with a dominant positive diagonal. `candidates`: each row lists distinct segment blocks of its own group, numbered 0 to 63 within the group, in its first 1 to 8 entries, then -1 in the rest; the rows of the node blocks of one group hold exactly 16 listed entries together (a block may appear in more than one row), and some row lists 8. `projection`: A segment of the node's own group: p // 128 lies in group * 64 to group * 64 + 63.
All inputs are finite; a program needn't handle non-finite values.
Results may differ from the reference program's by a relative error of at most 0.0026.
Values sent between devices are 32-bit elements; how exact they have to be, the bound alone decides.
A program may use at most 64 MiB of HBM per device.

```python
import math
import jax
import jax.numpy as jnp
from jax import lax

CX = 16
CY = 16
NZ = 128
BLK = 128
MAXC = 8
NX = 128
NY = 64
GROUPS = 8
GROUP_BLOCKS = 8
GROUP_SEGS = 64
NODE_BLOCKS = 64
SEGS = 65536
N_DOM = 8
N_SUB = 4


def plan_group(base_key, group_id):
    group_key = jax.random.fold_in(base_key, group_id)
    shuffled = jax.random.permutation(jax.random.fold_in(group_key, 1), GROUP_BLOCKS)
    position = jnp.argsort(shuffled)
    full_count = GROUP_BLOCKS // (MAXC - 1)
    remainder = GROUP_BLOCKS % (MAXC - 1)
    counts = jnp.where(position < full_count, MAXC, jnp.where(position == full_count, 1 + remainder, 1)).astype(jnp.int32)
    starts = jax.random.randint(jax.random.fold_in(group_key, 2), (GROUP_BLOCKS,), 0, GROUP_SEGS)
    starts = jnp.where(position == 0, GROUP_SEGS - MAXC + 1, starts).astype(jnp.int32)
    slot_ids = jnp.arange(MAXC)
    listed = (starts[:, None] + slot_ids[None, :]) % GROUP_SEGS
    lists = jnp.where(slot_ids[None, :] < counts[:, None], listed, -1).astype(jnp.int32)
    picked_slot = jax.random.randint(jax.random.fold_in(group_key, 3), (GROUP_BLOCKS, BLK), 0, counts[:, None])
    within = jax.random.randint(jax.random.fold_in(group_key, 4), (GROUP_BLOCKS, BLK), 0, BLK)
    lane_ids = jnp.arange(BLK)
    leading = (position == 0)[:, None]
    first_lane = leading & (lane_ids == 0)[None, :]
    second_lane = leading & (lane_ids == 1)[None, :]
    picked_slot = jnp.where(first_lane, MAXC - 2, jnp.where(second_lane, MAXC - 1, picked_slot))
    within = jnp.where(first_lane, BLK - 1, jnp.where(second_lane, 0, within))
    seg_blocks = jnp.take_along_axis(lists, picked_slot, axis=1)
    spare = (GROUP_SEGS - counts).astype(jnp.int32)
    stray_offset = jax.random.randint(jax.random.fold_in(group_key, 6), (GROUP_BLOCKS, BLK), 0, jnp.maximum(spare, 1)[:, None])
    stray_pick = jax.random.randint(jax.random.fold_in(group_key, 7), (GROUP_BLOCKS, BLK), 0, 4) == 0
    stray = stray_pick & (spare > 0)[:, None] & jnp.logical_not(first_lane | second_lane)
    stray_blocks = (starts[:, None] + counts[:, None] + stray_offset) % GROUP_SEGS
    seg_blocks = jnp.where(stray, stray_blocks, seg_blocks)
    targets = (group_id * GROUP_SEGS + seg_blocks) * BLK + within
    draws = jax.random.randint(jax.random.fold_in(group_key, 5), (GROUP_BLOCKS, BLK), 0, 4)
    flag_values = (draws != 0).astype(jnp.int32)
    return (lists, targets.astype(jnp.int32), flag_values)


def surface_plan(key):
    base_key = jax.random.fold_in(key, 17)
    group_ids = jnp.arange(GROUPS).astype(jnp.int32)
    lists, targets, flag_values = jax.vmap(lambda group_id: plan_group(base_key, group_id))(group_ids)
    return (lists.reshape(NODE_BLOCKS, MAXC), targets.reshape(NODE_BLOCKS, BLK), flag_values.reshape(NODE_BLOCKS, BLK))


def draw_candidates(key, part):
    return surface_plan(key)[0]


def draw_projection(key, part):
    return surface_plan(key)[1]


def draw_contact_flag(key, part):
    return surface_plan(key)[2]


def draw_element_stiffness(key, part):
    base_key = jax.random.fold_in(key, 11)
    factor = jax.random.truncated_normal(base_key, -3.0, 3.0, (24, 24), jnp.float32)
    matrix = jnp.dot(factor, factor.T) / 24.0 + 0.5 * jnp.eye(24, dtype=jnp.float32)
    return matrix.astype(jnp.bfloat16)


def shard_levels(key, dims, cuts, least, high):
    def one(axis_at, blocks):
        steps = jax.random.uniform(jax.random.fold_in(jax.random.fold_in(key, 6), axis_at), (blocks,), jnp.float32, least / len(cuts), high / len(cuts))
        return jnp.repeat(jnp.exp(steps), dims[axis_at] // blocks).reshape((-1,) + (1,) * (len(dims) - axis_at - 1))

    factor_of = one(*cuts[0])
    for cut in cuts[1:]:
        factor_of = factor_of * one(*cut)
    return factor_of


def noise(rng, dims, scale, bound, cuts=(), kind=jnp.bfloat16):
    values = jax.random.normal(rng, dims, jnp.float32) * scale
    if len(cuts) > 0:
        values = shard_levels(rng, dims, cuts, -0.22, 0.18) * values
    return jnp.clip(values, min=-bound, max=bound).astype(kind)


def setup_inputs(seed: int = 0) -> dict:
    seeds = jax.random.split(jax.random.key(seed), 13)
    displacement = noise(seeds[0], (3, NX, NY, NZ), 0.05, 0.3, ((1, 8), (2, 4)), jnp.float32)
    velocity = noise(seeds[1], (3, NX, NY, NZ), 1.0, 6.0, ((1, 8), (2, 4)), jnp.float32)
    modulus = jnp.clip(jnp.exp(math.log(4.0) - 2.0794415 * jax.random.uniform(seeds[2], (NX, NY, NZ), jnp.float32) ** shard_levels(seeds[2], (NX, NY, NZ), ((0, 8), (1, 4)), -0.2, 0.2)), 0.5, 4.0)
    element_stiffness = draw_element_stiffness(jax.random.fold_in(seeds[12], 71), 0)
    viscosity = jnp.clip(jax.random.uniform(seeds[4], (), jnp.float32, 0.1, 0.4), 0.1, 0.4)
    step_size = jnp.clip(jax.random.uniform(seeds[5], (), jnp.float32, 0.3, 0.6), 0.3, 0.6)
    seg_tilt = noise(seeds[6], (2, SEGS), 0.3, 1.5, ((1, 32),), jnp.float32)
    seg_offset = jnp.clip(-0.08 + 0.12 * jax.random.uniform(seeds[7], (SEGS,), jnp.float32) ** shard_levels(seeds[7], (SEGS,), ((0, 32),), -0.2, 0.2), -0.08, 0.04)
    seg_stiffness = jnp.clip(jnp.exp(math.log(40.0) - 2.3025851 * jax.random.uniform(seeds[8], (SEGS,), jnp.float32) ** shard_levels(seeds[8], (SEGS,), ((0, 32),), -0.2, 0.2)), 4.0, 40.0)
    projection = draw_projection(jax.random.fold_in(seeds[12], 71), 0)
    contact_flag = draw_contact_flag(jax.random.fold_in(seeds[12], 71), 0)
    candidates = draw_candidates(jax.random.fold_in(seeds[12], 71), 0)
    return dict(displacement=displacement, velocity=velocity, modulus=modulus, element_stiffness=element_stiffness, viscosity=viscosity, step_size=step_size, seg_tilt=seg_tilt, seg_offset=seg_offset, seg_stiffness=seg_stiffness, projection=projection, contact_flag=contact_flag, candidates=candidates)


def divergence_weights():
    entries = jnp.arange(24)
    component = entries // 8
    corner = entries % 8
    along = jnp.where(component == 0, corner // 4, jnp.where(component == 1, corner // 2 % 2, corner % 2))
    return (2.0 * along.astype(jnp.float32) - 1.0) * 0.25

def element_plane(fields, plane_index, row_count, first_x, first_y, total_x, total_y, stiffness, viscosity):
    layers = lax.dynamic_slice_in_dim(fields, plane_index, 2, 1)
    thickness = fields.shape[3]
    disp_parts = []
    speed_parts = []
    for corner_x in (0, 1):
        for corner_y in (0, 1):
            for corner_z in (0, 1):
                corner_rows = layers[:, corner_x, corner_y:corner_y + row_count, :]
                if corner_z:
                    corner_rows = jnp.roll(corner_rows, -1, axis=2)
                disp_parts.append(corner_rows[0:3])
                speed_parts.append(corner_rows[3:6])
    element_disp = jnp.stack(disp_parts, axis=1).reshape(24, row_count, thickness)
    element_speed = jnp.stack(speed_parts, axis=1).reshape(24, row_count, thickness)
    element_modulus = layers[6, 0, 0:row_count, :]
    global_x = first_x + plane_index
    global_y = first_y + jnp.arange(row_count)
    global_z = jnp.arange(thickness)
    inside_x = (global_x >= 0) & (global_x <= total_x - 2)
    inside_y = (global_y >= 0) & (global_y <= total_y - 2)
    inside = inside_x & inside_y[:, None] & (global_z <= thickness - 2)[None, :]
    weights = divergence_weights()
    volume_rate = lax.optimization_barrier(jnp.sum(weights[:, None, None] * element_speed, axis=0))
    bulk_visc = viscosity * jnp.maximum(-volume_rate, 0.0)
    combined = element_modulus[None] * element_disp + bulk_visc[None] * element_speed
    combined = jnp.where(inside[None], combined, 0.0).astype(jnp.bfloat16)
    element_force = jnp.dot(stiffness, combined.reshape(24, row_count * thickness), preferred_element_type=jnp.float32)
    return element_force.reshape(24, row_count, thickness)

def assemble(lower_force, upper_force):
    node_rows = lower_force.shape[1] - 1
    thickness = lower_force.shape[2]
    summed = jnp.zeros((3, node_rows, thickness), jnp.float32)
    for corner_x, element_force in ((1, lower_force), (0, upper_force)):
        grouped = element_force.reshape(3, 8, node_rows + 1, thickness)
        for corner_y in (0, 1):
            for corner_z in (0, 1):
                portion = grouped[:, corner_x * 4 + corner_y * 2 + corner_z, 1 - corner_y:1 - corner_y + node_rows, :]
                if corner_z:
                    portion = jnp.roll(portion, 1, axis=2)
                summed = summed + portion
    return summed

def margin_forces(fields, first_x, first_y, total_x, total_y, stiffness, viscosity):
    plane_count = fields.shape[1] - 2
    row_count = fields.shape[2] - 1

    def element_at(plane_index):
        return element_plane(fields, plane_index, row_count, first_x - 1, first_y - 1, total_x, total_y, stiffness, viscosity)

    def advance(lower_force, plane_index):
        upper_force = element_at(plane_index)
        return (upper_force, assemble(lower_force, upper_force))
    indices = jnp.arange(1, plane_count + 1).astype(jnp.int32)
    _, node_planes = lax.scan(advance, element_at(jnp.zeros((), jnp.int32)), indices)
    return jnp.transpose(node_planes, (1, 0, 2, 3))

def reference(displacement, velocity, modulus, element_stiffness, viscosity, step_size, seg_tilt, seg_offset, seg_stiffness, projection, contact_flag, candidates):
    fields = jnp.concatenate([displacement, velocity, modulus[None]], axis=0)
    fields = jnp.pad(fields, ((0, 0), (1, 1), (1, 1), (0, 0)))
    internal = margin_forces(fields, 0, 0, NX, NY, element_stiffness, viscosity)
    surface = jnp.transpose(displacement[:, :, :, NZ - 1].reshape(3, N_DOM, CX, N_SUB, CY), (0, 1, 3, 2, 4)).reshape(3, -1)
    targets = projection.reshape(-1)
    flag_values = contact_flag.reshape(-1)
    node_total = targets.shape[0]
    block_ids = jnp.arange(node_total) // BLK
    group_ids = block_ids // GROUP_BLOCKS
    target_block = targets // BLK - group_ids * GROUP_SEGS
    listed = jnp.any(candidates[block_ids] == target_block[:, None], axis=1)
    active = (flag_values == 1) & listed
    tilt_x = seg_tilt[0][targets]
    tilt_y = seg_tilt[1][targets]
    unit_scale = 1.0 / jnp.sqrt(1.0 + tilt_x * tilt_x + tilt_y * tilt_y)
    normal = jnp.stack([tilt_x * unit_scale, tilt_y * unit_scale, unit_scale])
    intersection = jnp.maximum(lax.optimization_barrier(jnp.sum(normal * surface, axis=0)) - seg_offset[targets], 0.0)
    pressure = jnp.where(active, seg_stiffness[targets] * intersection, 0.0)
    penalty_contact_load = pressure[None] * normal
    reaction = jax.ops.segment_sum(penalty_contact_load.T, targets, num_segments=SEGS).T
    load_grid = jnp.transpose(penalty_contact_load.reshape(3, N_DOM, N_SUB, CX, CY), (0, 1, 3, 2, 4)).reshape(3, NX, NY)
    total_force = -internal
    total_force = total_force.at[:, :, :, NZ - 1].add(-load_grid)
    new_velocity = velocity + step_size * total_force
    return (new_velocity, reaction)
```

```python
import functools

import jax
import jax.numpy as jnp
from jax import lax
from jax.experimental import pallas as pl
from jax.experimental.pallas import tpu as pltpu
from jax.sharding import PartitionSpec as P

MESH = pl.DeviceIdType.MESH
BLK = 128
UNROLL = 3
EARLY = 8
F32 = jnp.float32
BF16 = jnp.bfloat16
DIRS = tuple((dx, dy) for dx in (-1, 0, 1) for dy in (-1, 0, 1) if (dx, dy) != (0, 0))


def iota(shape, axis):
    return lax.broadcasted_iota(jnp.int32, shape, axis)


def split3(x):
    hi = x.astype(BF16)
    rest = x - hi.astype(F32)
    mid = rest.astype(BF16)
    low = (rest - mid.astype(F32)).astype(BF16)
    return hi, mid, low


def stiffness_maps(stiff):
    row = iota((96, 24), 0) // 8
    col = iota((96, 24), 1)
    wide = (iota((24, 192), 0) == iota((24, 192), 1) // 8).astype(BF16)
    parts = []
    for corner_y in (0, 1):
        pick = (col == (row // 2) * 4 + row % 2 + 2 * corner_y).astype(BF16)
        rows = jnp.dot(pick, stiff, preferred_element_type=F32).astype(BF16)
        parts.append(jnp.dot(rows, wide, preferred_element_type=F32))
    to_y = iota((96, 192), 0) % 8
    from_y = iota((96, 192), 1) % 8
    same = jnp.where(from_y == to_y, parts[0], 0.0) + jnp.where(from_y + 1 == to_y, parts[1], 0.0)
    carry = jnp.where((from_y == 7) & (to_y == 0), parts[1], 0.0)
    return same.astype(BF16), carry.astype(BF16)


def edge_maps(stiff, corner_y):
    row = iota((48, 24), 0) // 8
    col = iota((48, 24), 1)
    wide = (iota((24, 192), 0) == iota((24, 192), 1) // 8).astype(BF16)
    parts = []
    for corner_x in (0, 1):
        pick = (col == (row // 2) * 8 + row % 2 + 4 * corner_x + 2 * corner_y).astype(BF16)
        rows = jnp.dot(pick, stiff, preferred_element_type=F32).astype(BF16)
        parts.append(jnp.dot(rows, wide, preferred_element_type=F32))
    to_x = iota((48, 192), 0) % 8
    from_x = iota((48, 192), 1) % 8
    same = jnp.where(from_x == to_x, parts[1], 0.0) + jnp.where(from_x == to_x + 1, parts[0], 0.0)
    following = jnp.where((from_x == 0) & (to_x == 7), parts[0], 0.0)
    return same.astype(BF16), following.astype(BF16)


def kernel(
    dom_count, sub_count, visc_hbm, step_hbm, cand_hbm, stiff_hbm, tilt_hbm, off_hbm, stf_hbm, proj_hbm, flag_hbm,
    disp, vel, mod, nv_ref, react_ref, visc_ref, step_ref, cand_ref, stiff_ref, tilt_ref, proj_ref, flag_ref,
    w, xr, msg, nodes, back_out, back, table, values, same_ref, carry_ref, edge_ref, prev,
    local_sem, halo_send, halo_recv, peer_sem,
):
    d = lax.axis_index("dom")
    s = lax.axis_index("sub")
    planes, rows, nz = disp.shape[1], disp.shape[2], disp.shape[3]
    inner = slice(1, 1 + planes)
    seg_blocks = off_hbm.shape[0]
    node_blocks = proj_ref.shape[0]
    own = w.at[:, inner, 0:rows, :]
    stages = (
        ("stiff", ((stiff_hbm, stiff_ref),), stiff_ref),
        ("proj", ((proj_hbm, proj_ref),), proj_ref),
        ("flag", ((flag_hbm, flag_ref),), flag_ref),
        ("cand", ((cand_hbm, cand_ref),), cand_ref),
        ("disp", ((disp, own.at[0:3]),), own.at[0:3]),
        ("vel", ((vel, own.at[3:6]), (mod, own.at[6])), own.at[3:7]),
        ("tilt", ((tilt_hbm, tilt_ref),), tilt_ref),
        (
            "table",
            (
                (off_hbm, table.at[2 * seg_blocks : 3 * seg_blocks, :]),
                (stf_hbm, table.at[3 * seg_blocks : 4 * seg_blocks, :]),
            ),
            table.at[2 * seg_blocks : 4 * seg_blocks, :],
        ),
        ("visc", ((visc_hbm, visc_ref),), visc_ref),
        ("step", ((step_hbm, step_ref),), step_ref),
        (
            "rows",
            tuple(
                copy
                for k, y in ((1, 0), (2, rows - 1))
                for copy in (
                    (disp.at[:, :, y, :], xr.at[k, 0:3, inner, :]),
                    (vel.at[:, :, y, :], xr.at[k, 3:6, inner, :]),
                    (mod.at[:, y, :], xr.at[k, 6, inner, :]),
                )
            ),
            xr.at[1:3, :, inner, :],
        ),
    )
    waits = {}
    for i, (name, pairs, whole) in enumerate(stages):
        for a, b in pairs:
            pltpu.make_async_copy(a, b, local_sem.at[i]).start()
        waits[name] = pltpu.make_async_copy(whole, whole, local_sem.at[i])

    w[:, :, rows : rows + 8, :] = jnp.zeros((7, planes + 2, 8, nz), F32)
    for edge in (0, planes + 1):
        w[:, edge, 0:rows, :] = jnp.zeros((7, rows, nz), F32)
    for k in (0, 3):
        xr[k] = jnp.zeros(xr.shape[1:], F32)
    for k in (1, 2):
        xr[k, :, planes + 1 :, :] = jnp.zeros((7, xr.shape[2] - planes - 1, nz), F32)

    def exists(dx, dy):
        cond = (d + dx >= 0) & (d + dx < dom_count)
        return cond & (s + dy >= 0) & (s + dy < sub_count)

    barrier = pltpu.get_barrier_semaphore()
    for off in range(1, sub_count):
        pl.semaphore_signal(barrier, inc=1, device_id=(d, (s + off) % sub_count), device_id_type=MESH)
    for dx, dy in DIRS:
        if dx != 0:

            @pl.when(exists(dx, dy))
            def _():
                pl.semaphore_signal(barrier, inc=1, device_id=(d + dx, s + dy), device_id_type=MESH)

    waits["stiff"].wait()
    same, carry = stiffness_maps(stiff_ref[...])
    same_ref[...] = same
    carry_ref[...] = carry
    for k in (0, 1):
        same, following = edge_maps(stiff_ref[...], 1 - k)
        edge_ref[2 * k] = same
        edge_ref[2 * k + 1] = following

    for name in ("proj", "flag", "cand", "disp"):
        waits[name].wait()
    block_planes = BLK // rows
    group_start = d * (seg_blocks * BLK * sub_count)
    target = proj_ref[...] - group_start
    target_block = target // BLK
    listed = jnp.zeros(target.shape, jnp.bool_)
    for slot in range(cand_ref.shape[1]):
        listed = listed | (target_block == cand_ref[:, slot : slot + 1])
    chosen = jnp.where(listed & (flag_ref[...] == 1), target, -1).astype(F32)
    for c in range(3):
        for k in range(node_blocks):
            part = w[c, 1 + k * block_planes : 1 + (k + 1) * block_planes, 0:rows, :].reshape(BLK, nz)
            msg[c, k : k + 1, :] = jnp.transpose(part)[nz - 1 : nz, :]
    msg[3] = chosen

    columns = 1 + (s > 0).astype(jnp.int32) + (s < sub_count - 1).astype(jnp.int32)
    sides = (d > 0).astype(jnp.int32) + (d < dom_count - 1).astype(jnp.int32)
    pl.semaphore_wait(barrier, sub_count - 1 + columns * sides)

    def node_copy(off):
        return pltpu.make_async_remote_copy(
            src_ref=msg,
            dst_ref=nodes.at[:, node_blocks * off : node_blocks * (off + 1), :],
            send_sem=peer_sem.at[0],
            recv_sem=peer_sem.at[1],
            device_id=(d, (s + off) % sub_count),
            device_id_type=MESH,
        )

    for off in range(1, sub_count):
        node_copy(off).start()
    nodes_all = nodes.at[:, node_blocks : node_blocks * sub_count, :]
    waits["nodes_sent"] = pltpu.make_async_copy(nodes_all, nodes_all, peer_sem.at[0])
    waits["nodes"] = pltpu.make_async_copy(nodes_all, nodes_all, peer_sem.at[1])
    waits["vel"].wait()

    def halo_copy(dx, dy):
        src_x = {1: planes, -1: 1, 0: inner}[dx]
        dst_x = {1: 0, -1: planes + 1, 0: inner}[dx]
        if dy == 0:
            a, b = w.at[:, src_x, 0:rows, :], w.at[:, dst_x, 0:rows, :]
        else:
            a, b = w.at[:, src_x, rows - 1 if dy > 0 else 0, :], xr.at[0 if dy > 0 else 3, :, dst_x, :]
        return pltpu.make_async_remote_copy(
            src_ref=a,
            dst_ref=b,
            send_sem=halo_send.at[dx + 1],
            recv_sem=halo_recv.at[dx + 1],
            device_id=(d + dx, s + dy),
            device_id_type=MESH,
        )

    for dx, dy in DIRS:

        @pl.when(exists(dx, dy))
        def _():
            halo_copy(dx, dy).start()

    def halo_wait(sem, sign):
        both = (s > 0) & (s < sub_count - 1)
        for dx in (-1, 0, 1):
            for many, present in ((2, both), (1, jnp.logical_not(both))):
                if dx == 0:
                    part = w.at[:, 0:planes, 0:many, :]
                else:
                    part = w.at[:, 0 : rows + many, 0, :]

                @pl.when(present & exists(sign * dx, 0))
                def _():
                    pltpu.make_async_copy(part, part, sem.at[dx + 1]).wait()

    nodes[:, 0:node_blocks, :] = msg[...]
    for name in ("tilt", "table", "visc", "step"):
        waits[name].wait()
    for b in range(seg_blocks):
        lanes = slice(b * BLK, (b + 1) * BLK)
        for c in range(2):
            table[c * seg_blocks + b : c * seg_blocks + b + 1, :] = tilt_ref[c : c + 1, lanes]
    table3 = jnp.concatenate(split3(table[...]), axis=0)

    viscosity = visc_ref[0]
    step = step_ref[0]
    row_blocks = rows // 8

    def element_blocks(view, modulus, mask):
        def corner_views(field, a):
            flat = [view(field, a, b) for b in (0, 1)]
            return [[x, pltpu.roll(x, nz - 1, 1)] for x in flat]

        speed = [[corner_views(3 + m, a) for a in (0, 1)] for m in range(3)]
        rate = None
        for m in range(3):
            for a in (0, 1):
                for b in (0, 1):
                    for c in (0, 1):
                        term = speed[m][a][b][c]
                        sign = (a, b, c)[m]
                        if rate is None:
                            rate = -term
                        else:
                            rate = rate + term if sign else rate - term
        bulk = (viscosity * mask) * jnp.maximum(-0.25 * rate, 0.0)
        factor = mask * modulus
        entries = []
        for m in range(3):
            for a in (0, 1):
                disps = corner_views(m, a)
                for b in (0, 1):
                    for c in (0, 1):
                        entries.append(factor * disps[b][c] + bulk * speed[m][a][b][c])
        return [
            jnp.concatenate([x[8 * t : 8 * t + 8, :] for x in entries], axis=0).astype(BF16)
            for t in range(entries[0].shape[0] // 8)
        ]

    def mapped(map_ref, blocks):
        wide = jnp.dot(map_ref[...], jnp.concatenate(blocks, axis=1), preferred_element_type=F32)
        return [wide[:, t * nz : (t + 1) * nz] for t in range(len(blocks))]

    inside_yz = ((iota((rows, nz), 0) <= rows - 2) & (iota((rows, nz), 1) <= nz - 2)).astype(F32)

    def element_plane(e, mask):
        blocks = element_blocks(lambda f, a, b: w[f, e + a, b : b + rows, :], w[6, e, 0:rows, :], mask)
        force = mapped(same_ref, blocks)
        carried = mapped(carry_ref, blocks[:-1]) if row_blocks > 1 else []
        return [force[0]] + [x + y for x, y in zip(force[1:], carried)]

    def part_of(force, m, a, c):
        at = ((m * 2 + a) * 2 + c) * 8
        return force[at : at + 8, :]

    def node_plane(e, force):
        for m in range(3):
            for t in range(row_blocks):
                part = [part_of(force[t], m, 0, c) + prev[m * 2 + c, t] for c in (0, 1)]
                internal = part[0] + pltpu.roll(part[1], 1, 1)
                at = slice(8 * t, 8 * t + 8)
                nv_ref[m, e - 1, at, :] = w[3 + m, e, at, :] - step * internal

    def advance(e):
        force = element_plane(e, inside_yz)
        node_plane(e, force)
        for m in range(3):
            for c in (0, 1):
                for t in range(row_blocks):
                    prev[m * 2 + c, t] = part_of(force[t], m, 1, c)

    prev[...] = jnp.zeros(prev.shape, F32)
    group = UNROLL if (planes - 1) % UNROLL == 0 else 1
    early = (planes - 1) // group * EARLY // 16

    def advance_group(g):
        for i in range(group):
            advance(1 + g * group + i)

    @pl.loop(0, early)
    def _(g):
        advance_group(g)

    waits["nodes"].wait()

    group_rows = node_blocks * sub_count
    wanted = nodes[3].astype(jnp.int32) - s * (seg_blocks * BLK)
    valid = (nodes[3] >= 0.0) & (wanted >= 0) & (wanted < seg_blocks * BLK)
    wanted = jnp.where(valid, wanted, 0)
    lane = wanted % BLK
    block = jnp.where(valid, wanted // BLK, -1)
    lane_rows = iota((BLK, BLK), 0)
    block_rows = iota((seg_blocks, BLK), 0)
    hot = jnp.concatenate(
        [(lane_rows == lane[r : r + 1, :]).astype(F32).astype(BF16) for r in range(group_rows)], axis=1
    )
    in_block = [block_rows == block[r : r + 1, :] for r in range(group_rows)]
    found = jnp.dot(table3, hot, preferred_element_type=F32)
    count = 4 * seg_blocks
    found = found[0:count] + found[count : 2 * count] + found[2 * count : 3 * count]
    for f in range(4):
        field = found[f * seg_blocks : (f + 1) * seg_blocks]
        for r in range(group_rows):
            picked = jnp.where(in_block[r], field[:, r * BLK : (r + 1) * BLK], 0.0)
            values[f, r : r + 1, :] = jnp.sum(picked, axis=0, keepdims=True)
    tilt_x, tilt_y = values[0], values[1]
    unit = 1.0 / jnp.sqrt(1.0 + tilt_x * tilt_x + tilt_y * tilt_y)
    normal = (tilt_x * unit, tilt_y * unit, unit)
    depth = normal[0] * nodes[0] + normal[1] * nodes[1] + normal[2] * nodes[2] - values[2]
    pressure = jnp.where(valid, values[3] * jnp.maximum(depth, 0.0), 0.0)
    loads = [pressure * n for n in normal]
    for c in range(3):
        back_out[c] = loads[c]
    spread = jnp.concatenate(
        [
            jnp.concatenate([jnp.where(in_block[r], loads[c][r : r + 1, :], 0.0) for r in range(group_rows)], axis=1)
            for c in range(3)
        ],
        axis=0,
    )
    high = spread.astype(BF16)
    low = (spread - high.astype(F32)).astype(BF16)
    summed = lax.dot_general(
        jnp.concatenate([high, low], axis=0), hot, (((1,), (1,)), ((), ())), preferred_element_type=F32
    )
    summed = summed[0 : 3 * seg_blocks] + summed[3 * seg_blocks :]
    for c in range(3):
        for b in range(seg_blocks):
            at = c * seg_blocks + b
            react_ref[c : c + 1, b * BLK : (b + 1) * BLK] = summed[at : at + 1, :]

    def load_copy(off):
        return pltpu.make_async_remote_copy(
            src_ref=back_out.at[:, node_blocks * off : node_blocks * (off + 1), :],
            dst_ref=back.at[:, node_blocks * (off - 1) : node_blocks * off, :],
            send_sem=peer_sem.at[2],
            recv_sem=peer_sem.at[3],
            device_id=(d, (s + sub_count - off) % sub_count),
            device_id_type=MESH,
        )

    for off in range(1, sub_count):
        load_copy(off).start()

    @pl.loop(early, (planes - 1) // group)
    def _(g):
        advance_group(g)

    waits["rows"].wait()
    halo_wait(halo_recv, -1)

    for k, y in ((1, 0), (2, rows - 1)):
        for edge in (0, planes + 1):
            xr[k, :, edge, :] = w[:, edge, y, :]

    node_plane(planes, element_plane(planes, inside_yz * (d < dom_count - 1).astype(F32)))
    force = element_plane(0, inside_yz * (d > 0).astype(F32))
    for m in range(3):
        for t in range(row_blocks):
            internal = part_of(force[t], m, 1, 0) + pltpu.roll(part_of(force[t], m, 1, 1), 1, 1)
            at = slice(8 * t, 8 * t + 8)
            nv_ref[m, 0, at, :] = nv_ref[m, 0, at, :] - step * internal

    height = planes + 8
    global_x = d * planes - 1 + iota((height, nz), 0)
    inside_xz = (
        (global_x >= 0) & (global_x <= planes * dom_count - 2) & (iota((height, nz), 1) <= nz - 2)
    ).astype(F32)
    for k, y, present in ((0, 0, s > 0), (1, rows - 1, s < sub_count - 1)):
        blocks = element_blocks(
            lambda f, a, b: xr[2 * k + b, f, a : a + height, :], xr[2 * k, 6, 0:height, :], inside_xz * present.astype(F32)
        )
        here = mapped(edge_ref.at[2 * k], blocks[:-1])
        after = mapped(edge_ref.at[2 * k + 1], blocks[1:])
        for t in range(planes // 8):
            force = here[t] + after[t]
            for m in range(3):
                at = m * 16
                internal = step * (force[at : at + 8, :] + pltpu.roll(force[at + 8 : at + 16, :], 1, 1))
                for j in range(8):
                    x = 8 * t + j
                    nv_ref[m, x, y : y + 1, :] = nv_ref[m, x, y : y + 1, :] - internal[j : j + 1, :]

    pltpu.make_async_copy(back, back, peer_sem.at[3]).wait()
    top = iota((nz, BLK), 0) == nz - 1
    for c in range(3):
        total = back_out[c, 0:node_blocks, :]
        for off in range(1, sub_count):
            total = total + back[c, node_blocks * (off - 1) : node_blocks * off, :]
        total = step * total
        for k in range(node_blocks):
            column = jnp.transpose(jnp.where(top, total[k : k + 1, :], 0.0)).reshape(block_planes, rows, nz)
            at = slice(k * block_planes, (k + 1) * block_planes)
            nv_ref[c, at, :, :] = nv_ref[c, at, :, :] - column

    waits["nodes_sent"].wait()
    pltpu.make_async_copy(back, back, peer_sem.at[2]).wait()
    halo_wait(halo_send, 1)


def store_kernel(nv_ref, react_ref, nv_out, react_out, sem):
    copies = [
        pltpu.make_async_copy(a, b, sem.at[i]) for i, (a, b) in enumerate(((nv_ref, nv_out), (react_ref, react_out)))
    ]
    for copy in copies:
        copy.start()
    for copy in copies:
        copy.wait()


def local(
    dom_count, sub_count, displacement, velocity, modulus, element_stiffness, viscosity, step_size, seg_tilt,
    seg_offset, seg_stiffness, projection, contact_flag, candidates,
):
    _, planes, rows, nz = displacement.shape
    seg_local = seg_offset.shape[0]
    seg_blocks = seg_local // BLK
    node_blocks = projection.shape[0]
    group_rows = node_blocks * sub_count
    peers = sub_count - 1
    vmem = pl.BlockSpec(memory_space=pltpu.VMEM)
    hbm = pl.BlockSpec(memory_space=pl.ANY)
    dma = pltpu.SemaphoreType.DMA
    results = pl.pallas_call(
        functools.partial(kernel, dom_count, sub_count),
        out_shape=(
            pltpu.VMEM(velocity.shape, F32),
            pltpu.VMEM((3, seg_local), F32),
        ),
        in_specs=[hbm] * 12,
        out_specs=(vmem, vmem),
        scratch_shapes=[
            pltpu.SMEM((1,), F32),
            pltpu.SMEM((1,), F32),
            pltpu.VMEM(candidates.shape, jnp.int32),
            pltpu.VMEM(element_stiffness.shape, BF16),
            pltpu.VMEM(seg_tilt.shape, F32),
            pltpu.VMEM(projection.shape, jnp.int32),
            pltpu.VMEM(contact_flag.shape, jnp.int32),
            pltpu.VMEM((7, planes + 2, rows + 8, nz), F32),
            pltpu.VMEM((4, 7, planes + 16, nz), F32),
            pltpu.VMEM((4, node_blocks, BLK), F32),
            pltpu.VMEM((4, group_rows, BLK), F32),
            pltpu.VMEM((3, group_rows, BLK), F32),
            pltpu.VMEM((3, node_blocks * peers, BLK), F32),
            pltpu.VMEM((4 * seg_blocks, BLK), F32),
            pltpu.VMEM((4, group_rows, BLK), F32),
            pltpu.VMEM((96, 192), BF16),
            pltpu.VMEM((96, 192), BF16),
            pltpu.VMEM((4, 48, 192), BF16),
            pltpu.VMEM((6, rows // 8, 8, nz), F32),
            dma((11,)),
            dma((3,)),
            dma((3,)),
            dma((4,)),
        ],
        compiler_params=pltpu.CompilerParams(collective_id=0, has_side_effects=True),
    )(
        viscosity.reshape(1),
        step_size.reshape(1),
        candidates,
        element_stiffness,
        seg_tilt,
        seg_offset.reshape(seg_blocks, BLK),
        seg_stiffness.reshape(seg_blocks, BLK),
        projection,
        contact_flag,
        displacement,
        velocity,
        modulus,
    )
    return pl.pallas_call(
        store_kernel,
        out_shape=tuple(jax.ShapeDtypeStruct(x.shape, F32) for x in results),
        in_specs=[vmem, vmem],
        out_specs=(hbm, hbm),
        scratch_shapes=[dma((2,))],
    )(*(pltpu.with_memory_space_constraint(x, pltpu.VMEM) for x in results))


def solution(mesh):
    return jax.shard_map(
        functools.partial(local, mesh.shape["dom"], mesh.shape["sub"]),
        mesh=mesh,
        in_specs=(
            P(None, "dom", "sub", None),
            P(None, "dom", "sub", None),
            P("dom", "sub", None),
            P(),
            P(),
            P(),
            P(None, ("dom", "sub")),
            P(("dom", "sub")),
            P(("dom", "sub")),
            P(("dom", "sub"), None),
            P(("dom", "sub"), None),
            P(("dom", "sub"), None),
        ),
        out_specs=(P(None, "dom", "sub", None), P(None, ("dom", "sub"))),
        check_vma=False,
    )
```

```python
import functools

import jax
import jax.numpy as jnp
from jax import lax
from jax.experimental import pallas as pl
from jax.experimental.pallas import tpu as pltpu
from jax.sharding import PartitionSpec as P

MESH = pl.DeviceIdType.MESH
BLK = 128
UNROLL = 3
F32 = jnp.float32
BF16 = jnp.bfloat16
DIRS = tuple((dx, dy) for dx in (-1, 0, 1) for dy in (-1, 0, 1) if (dx, dy) != (0, 0))


def iota(shape, axis):
    return lax.broadcasted_iota(jnp.int32, shape, axis)


def split3(x):
    hi = x.astype(BF16)
    rest = x - hi.astype(F32)
    mid = rest.astype(BF16)
    low = (rest - mid.astype(F32)).astype(BF16)
    return hi, mid, low


def stiffness_maps(stiff):
    row = iota((96, 24), 0) // 8
    col = iota((96, 24), 1)
    wide = (iota((24, 192), 0) == iota((24, 192), 1) // 8).astype(BF16)
    parts = []
    for corner_y in (0, 1):
        pick = (col == (row // 2) * 4 + row % 2 + 2 * corner_y).astype(BF16)
        rows = jnp.dot(pick, stiff, preferred_element_type=F32).astype(BF16)
        parts.append(jnp.dot(rows, wide, preferred_element_type=F32))
    to_y = iota((96, 192), 0) % 8
    from_y = iota((96, 192), 1) % 8
    same = jnp.where(from_y == to_y, parts[0], 0.0) + jnp.where(from_y + 1 == to_y, parts[1], 0.0)
    carry = jnp.where((from_y == 7) & (to_y == 0), parts[1], 0.0)
    return same.astype(BF16), carry.astype(BF16)


def edge_maps(stiff, corner_y):
    row = iota((48, 24), 0) // 8
    col = iota((48, 24), 1)
    wide = (iota((24, 192), 0) == iota((24, 192), 1) // 8).astype(BF16)
    parts = []
    for corner_x in (0, 1):
        pick = (col == (row // 2) * 8 + row % 2 + 4 * corner_x + 2 * corner_y).astype(BF16)
        rows = jnp.dot(pick, stiff, preferred_element_type=F32).astype(BF16)
        parts.append(jnp.dot(rows, wide, preferred_element_type=F32))
    to_x = iota((48, 192), 0) % 8
    from_x = iota((48, 192), 1) % 8
    same = jnp.where(from_x == to_x, parts[1], 0.0) + jnp.where(from_x == to_x + 1, parts[0], 0.0)
    following = jnp.where((from_x == 0) & (to_x == 7), parts[0], 0.0)
    return same.astype(BF16), following.astype(BF16)


def kernel(
    dom_count, sub_count, visc_hbm, step_hbm, cand_hbm, stiff_hbm, tilt_hbm, off_hbm, stf_hbm, proj_hbm, flag_hbm,
    disp, vel, mod, nv_ref, react_ref, visc_ref, step_ref, cand_ref, stiff_ref, tilt_ref, proj_ref, flag_ref,
    w, xr, xc, msg, nodes, tables, values, own_values, same_ref, carry_ref, edge_ref, prev,
    local_sem, halo_send, halo_recv, peer_sem,
):
    d = lax.axis_index("dom")
    s = lax.axis_index("sub")
    planes, rows, nz = disp.shape[1], disp.shape[2], disp.shape[3]
    inner = slice(1, 1 + planes)
    table = tables.at[0]
    seg_blocks = off_hbm.shape[0]
    node_blocks = proj_ref.shape[0]
    def exists(dx, dy):
        cond = (d + dx >= 0) & (d + dx < dom_count)
        return cond & (s + dy >= 0) & (s + dy < sub_count)

    xc[...] = jnp.zeros(xc.shape, F32)
    barrier = pltpu.get_barrier_semaphore()
    for off in range(1, sub_count):
        pl.semaphore_signal(barrier, inc=1, device_id=(d, (s + off) % sub_count), device_id_type=MESH)
    for dx, dy in DIRS:
        if dx != 0:

            @pl.when(exists(dx, dy))
            def _():
                pl.semaphore_signal(barrier, inc=1, device_id=(d + dx, s + dy), device_id_type=MESH)

    own = w.at[:, inner, 0:rows, :]
    stages = (
        ("stiff", ((stiff_hbm, stiff_ref),), stiff_ref),
        ("proj", ((proj_hbm, proj_ref),), proj_ref),
        ("flag", ((flag_hbm, flag_ref),), flag_ref),
        ("cand", ((cand_hbm, cand_ref),), cand_ref),
        ("disp", ((disp, own.at[0:3]),), own.at[0:3]),
        ("vel", ((vel, own.at[3:6]), (mod, own.at[6])), own.at[3:7]),
        ("tilt", ((tilt_hbm, tilt_ref),), tilt_ref),
        (
            "table",
            (
                (off_hbm, table.at[2 * seg_blocks : 3 * seg_blocks, :]),
                (stf_hbm, table.at[3 * seg_blocks : 4 * seg_blocks, :]),
            ),
            table.at[2 * seg_blocks : 4 * seg_blocks, :],
        ),
        ("visc", ((visc_hbm, visc_ref),), visc_ref),
        ("step", ((step_hbm, step_ref),), step_ref),
        (
            "rows",
            tuple(
                copy
                for k, y in ((1, 0), (2, rows - 1))
                for copy in (
                    (disp.at[:, :, y, :], xr.at[k, 0:3, inner, :]),
                    (vel.at[:, :, y, :], xr.at[k, 3:6, inner, :]),
                    (mod.at[:, y, :], xr.at[k, 6, inner, :]),
                )
            ),
            xr.at[1:3, :, inner, :],
        ),
    )
    waits = {}
    for i, (name, pairs, whole) in enumerate(stages):
        for a, b in pairs:
            pltpu.make_async_copy(a, b, local_sem.at[i]).start()
        waits[name] = pltpu.make_async_copy(whole, whole, local_sem.at[i])

    w[:, :, rows : rows + 8, :] = jnp.zeros((7, planes + 2, 8, nz), F32)
    for k in (0, 1, 2, 3):
        xr[k, :, 0:1, :] = jnp.zeros((7, 1, nz), F32)
        xr[k, :, planes + 1 :, :] = jnp.zeros((7, xr.shape[2] - planes - 1, nz), F32)
    for dx, edge in ((1, 0), (-1, planes + 1)):

        @pl.when(jnp.logical_not(exists(-dx, 0)))
        def _():
            w[:, edge, 0:rows, :] = jnp.zeros((7, rows, nz), F32)

    for dy, k in ((1, 0), (-1, 3)):

        @pl.when(jnp.logical_not(exists(0, -dy)))
        def _():
            xr[k, :, 1 : planes + 1, :] = jnp.zeros((7, planes, nz), F32)

    waits["stiff"].wait()
    same, carry = stiffness_maps(stiff_ref[...])
    same_ref[...] = same
    carry_ref[...] = carry
    for k in (0, 1):
        same, following = edge_maps(stiff_ref[...], 1 - k)
        edge_ref[2 * k] = same
        edge_ref[2 * k + 1] = following

    for name in ("proj", "flag", "cand", "disp"):
        waits[name].wait()
    block_planes = BLK // rows
    group_start = d * (seg_blocks * BLK * sub_count)
    target = proj_ref[...] - group_start
    target_block = target // BLK
    listed = jnp.zeros(target.shape, jnp.bool_)
    for slot in range(cand_ref.shape[1]):
        listed = listed | (target_block == cand_ref[:, slot : slot + 1])
    chosen = jnp.where(listed & (flag_ref[...] == 1), target, -1).astype(F32)
    for c in range(3):
        for k in range(node_blocks):
            part = w[c, 1 + k * block_planes : 1 + (k + 1) * block_planes, 0:rows, :].reshape(BLK, nz)
            msg[c, k : k + 1, :] = jnp.transpose(part)[nz - 1 : nz, :]
    msg[3] = chosen

    for name in ("tilt", "table", "visc", "step"):
        waits[name].wait()
    for b in range(seg_blocks):
        lanes = slice(b * BLK, (b + 1) * BLK)
        for c in range(2):
            table[c * seg_blocks + b : c * seg_blocks + b + 1, :] = tilt_ref[c : c + 1, lanes]
    columns = 1 + (s > 0).astype(jnp.int32) + (s < sub_count - 1).astype(jnp.int32)
    sides = (d > 0).astype(jnp.int32) + (d < dom_count - 1).astype(jnp.int32)
    pl.semaphore_wait(barrier, sub_count - 1 + columns * sides)

    waits["vel"].wait()

    def halo_copy(dx, dy):
        src_x = {1: planes, -1: 1, 0: inner}[dx]
        dst_x = {1: 0, -1: planes + 1, 0: inner}[dx]
        if dy == 0:
            a, b = w.at[:, src_x, 0:rows, :], w.at[:, dst_x, 0:rows, :]
        else:
            k = 0 if dy > 0 else 3
            a = w.at[:, src_x, rows - 1 if dy > 0 else 0, :]
            b = xr.at[k, :, inner, :] if dx == 0 else xc.at[k, :, 0 if dx > 0 else 3, :]
        return pltpu.make_async_remote_copy(
            src_ref=a,
            dst_ref=b,
            send_sem=halo_send.at[dx + 1],
            recv_sem=halo_recv.at[dx + 1],
            device_id=(d + dx, s + dy),
            device_id_type=MESH,
        )

    def send_halo(dirs):
        for dx, dy in dirs:

            @pl.when(exists(dx, dy))
            def _():
                halo_copy(dx, dy).start()

    send_halo([(dx, dy) for dx, dy in DIRS if dy == 0])

    def node_copy(off):
        return pltpu.make_async_remote_copy(
            src_ref=msg,
            dst_ref=nodes.at[:, node_blocks * off : node_blocks * (off + 1), :],
            send_sem=peer_sem.at[0],
            recv_sem=peer_sem.at[1],
            device_id=(d, (s + off) % sub_count),
            device_id_type=MESH,
        )

    for off in range(1, sub_count):
        node_copy(off).start()
    send_halo([(dx, dy) for dx, dy in DIRS if dy != 0])

    def table_copy(off):
        return pltpu.make_async_remote_copy(
            src_ref=table,
            dst_ref=tables.at[off],
            send_sem=peer_sem.at[2],
            recv_sem=peer_sem.at[3],
            device_id=(d, (s + off) % sub_count),
            device_id_type=MESH,
        )

    for off in range(1, sub_count):
        table_copy(off).start()
    received = tables.at[1:sub_count]
    waits["tables_sent"] = pltpu.make_async_copy(received, received, peer_sem.at[2])
    waits["tables"] = pltpu.make_async_copy(received, received, peer_sem.at[3])
    nodes_all = nodes.at[:, node_blocks : node_blocks * sub_count, :]
    waits["nodes_sent"] = pltpu.make_async_copy(nodes_all, nodes_all, peer_sem.at[0])
    waits["nodes"] = pltpu.make_async_copy(nodes_all, nodes_all, peer_sem.at[1])
    def halo_wait(sem, sign, sides):
        both = (s > 0) & (s < sub_count - 1)
        for dx in sides:
            for many, present in ((2, both), (1, jnp.logical_not(both))):
                if dx == 0:
                    part = w.at[:, 0:planes, 0:many, :]
                else:
                    part = w.at[:, 0 : rows + many, 0, :]

                @pl.when(present & exists(sign * dx, 0))
                def _():
                    pltpu.make_async_copy(part, part, sem.at[dx + 1]).wait()

    nodes[:, 0:node_blocks, :] = msg[...]
    viscosity = visc_ref[0]
    step = step_ref[0]
    row_blocks = rows // 8

    def element_blocks(view, modulus, mask):
        def corner_views(field, a):
            flat = [view(field, a, b) for b in (0, 1)]
            return [[x, pltpu.roll(x, nz - 1, 1)] for x in flat]

        speed = [[corner_views(3 + m, a) for a in (0, 1)] for m in range(3)]
        rate = None
        for m in range(3):
            for a in (0, 1):
                for b in (0, 1):
                    for c in (0, 1):
                        term = speed[m][a][b][c]
                        sign = (a, b, c)[m]
                        if rate is None:
                            rate = -term
                        else:
                            rate = rate + term if sign else rate - term
        bulk = (viscosity * mask) * jnp.maximum(-0.25 * rate, 0.0)
        factor = mask * modulus
        entries = []
        for m in range(3):
            for a in (0, 1):
                disps = corner_views(m, a)
                for b in (0, 1):
                    for c in (0, 1):
                        entries.append(factor * disps[b][c] + bulk * speed[m][a][b][c])
        return [
            jnp.concatenate([x[8 * t : 8 * t + 8, :] for x in entries], axis=0).astype(BF16)
            for t in range(entries[0].shape[0] // 8)
        ]

    def mapped(map_ref, blocks):
        wide = jnp.dot(map_ref[...], jnp.concatenate(blocks, axis=1), preferred_element_type=F32)
        return [wide[:, t * nz : (t + 1) * nz] for t in range(len(blocks))]

    inside_yz = ((iota((rows, nz), 0) <= rows - 2) & (iota((rows, nz), 1) <= nz - 2)).astype(F32)

    def element_plane(e, mask):
        blocks = element_blocks(lambda f, a, b: w[f, e + a, b : b + rows, :], w[6, e, 0:rows, :], mask)
        force = mapped(same_ref, blocks)
        carried = mapped(carry_ref, blocks[:-1]) if row_blocks > 1 else []
        return [force[0]] + [x + y for x, y in zip(force[1:], carried)]

    def part_of(force, m, a, c):
        at = ((m * 2 + a) * 2 + c) * 8
        return force[at : at + 8, :]

    def node_plane(e, force):
        for m in range(3):
            for t in range(row_blocks):
                part = [part_of(force[t], m, 0, c) + prev[m * 2 + c, t] for c in (0, 1)]
                internal = part[0] + pltpu.roll(part[1], 1, 1)
                at = slice(8 * t, 8 * t + 8)
                nv_ref[m, e - 1, at, :] = w[3 + m, e, at, :] - step * internal

    def advance(e):
        force = element_plane(e, inside_yz)
        node_plane(e, force)
        for m in range(3):
            for c in (0, 1):
                for t in range(row_blocks):
                    prev[m * 2 + c, t] = part_of(force[t], m, 1, c)

    prev[...] = jnp.zeros(prev.shape, F32)
    group = UNROLL if (planes - 1) % UNROLL == 0 else 1

    def advance_group(g):
        for i in range(group):
            advance(1 + g * group + i)

    @pl.loop(0, (planes - 1) // group)
    def _(g):
        advance_group(g)

    for m in range(3):
        for t in range(row_blocks):
            internal = prev[m * 2, t] + pltpu.roll(prev[m * 2 + 1, t], 1, 1)
            at = slice(8 * t, 8 * t + 8)
            nv_ref[m, planes - 1, at, :] = w[3 + m, planes, at, :] - step * internal

    waits["nodes"].wait()

    group_rows = node_blocks * sub_count
    lane_rows = iota((BLK, BLK), 0)

    def one_hot(lane):
        return jnp.concatenate(
            [(lane_rows == lane[r : r + 1, :]).astype(F32).astype(BF16) for r in range(lane.shape[0])], axis=1
        )

    def contact(slots, store, hot, in_block, valid, place):
        parts = jnp.concatenate(split3(tables[0:slots].reshape(slots * 4 * seg_blocks, BLK)), axis=0)
        found = jnp.dot(parts, hot, preferred_element_type=F32)
        count = slots * 4 * seg_blocks
        found = found[0:count] + found[count : 2 * count] + found[2 * count : 3 * count]
        for f in range(4):
            for r in range(len(in_block)):
                picked = None
                for k in range(slots):
                    at = (k * 4 + f) * seg_blocks
                    field = found[at : at + seg_blocks, r * BLK : (r + 1) * BLK]
                    term = jnp.where(in_block[r][k * seg_blocks : (k + 1) * seg_blocks], field, 0.0)
                    picked = term if picked is None else picked + term
                store[f, r : r + 1, :] = jnp.sum(picked, axis=0, keepdims=True)
        tilt_x, tilt_y = store[0], store[1]
        unit = 1.0 / jnp.sqrt(1.0 + tilt_x * tilt_x + tilt_y * tilt_y)
        normal = (tilt_x * unit, tilt_y * unit, unit)
        depth = normal[0] * place[0] + normal[1] * place[1] + normal[2] * place[2] - store[2]
        pressure = jnp.where(valid, store[3] * jnp.maximum(depth, 0.0), 0.0)
        return [pressure * n for n in normal]

    wanted = nodes[3].astype(jnp.int32) - s * (seg_blocks * BLK)
    valid = (nodes[3] >= 0.0) & (wanted >= 0) & (wanted < seg_blocks * BLK)
    wanted = jnp.where(valid, wanted, 0)
    block = jnp.where(valid, wanted // BLK, -1)
    hot = one_hot(wanted % BLK)
    block_rows = iota((seg_blocks, BLK), 0)
    in_block = [block_rows == block[r : r + 1, :] for r in range(group_rows)]
    loads = contact(1, values, hot, in_block, valid, nodes)
    spread = jnp.concatenate(
        [
            jnp.concatenate([jnp.where(in_block[r], loads[c][r : r + 1, :], 0.0) for r in range(group_rows)], axis=1)
            for c in range(3)
        ],
        axis=0,
    )
    high = spread.astype(BF16)
    low = (spread - high.astype(F32)).astype(BF16)
    summed = lax.dot_general(
        jnp.concatenate([high, low], axis=0), hot, (((1,), (1,)), ((), ())), preferred_element_type=F32
    )
    summed = summed[0 : 3 * seg_blocks] + summed[3 * seg_blocks :]
    for c in range(3):
        for b in range(seg_blocks):
            at = c * seg_blocks + b
            react_ref[c : c + 1, b * BLK : (b + 1) * BLK] = summed[at : at + 1, :]

    waits["rows"].wait()
    halo_wait(halo_recv, -1, (0,))
    sides = ((0, 0, s > 0), (1, rows - 1, s < sub_count - 1))
    along = iota((planes, nz), 0)
    inside_xz = ((along >= 1) & (iota((planes, nz), 1) <= nz - 2)).astype(F32)
    for k, y, present in sides:
        blocks = element_blocks(
            lambda f, a, b: xr[2 * k + b, f, a : a + planes, :],
            xr[2 * k, 6, 0:planes, :],
            inside_xz * present.astype(F32),
        )
        here = mapped(edge_ref.at[2 * k], blocks)
        after = mapped(edge_ref.at[2 * k + 1], blocks[1:]) if planes > 8 else []
        for t in range(planes // 8):
            force = here[t] + after[t] if t < len(after) else here[t]
            for m in range(3):
                at = m * 16
                internal = step * (force[at : at + 8, :] + pltpu.roll(force[at + 8 : at + 16, :], 1, 1))
                for j in range(8):
                    x = 8 * t + j
                    nv_ref[m, x, y : y + 1, :] = nv_ref[m, x, y : y + 1, :] - internal[j : j + 1, :]

    own_valid = msg[3] >= 0.0
    own_wanted = jnp.where(own_valid, msg[3].astype(jnp.int32), 0)
    slot = (s + sub_count - own_wanted // (seg_blocks * BLK)) % sub_count
    own_block = slot * seg_blocks + own_wanted % (seg_blocks * BLK) // BLK
    own_block = jnp.where(own_valid, own_block, -1)
    own_hot = one_hot(own_wanted % BLK)
    own_rows = iota((sub_count * seg_blocks, BLK), 0)
    own_in_block = [own_rows == own_block[r : r + 1, :] for r in range(node_blocks)]
    waits["tables"].wait()
    loads = contact(sub_count, own_values, own_hot, own_in_block, own_valid, msg)
    top = iota((nz, BLK), 0) == nz - 1
    for c in range(3):
        total = step * loads[c]
        for k in range(node_blocks):
            column = jnp.transpose(jnp.where(top, total[k : k + 1, :], 0.0)).reshape(block_planes, rows, nz)
            at = slice(k * block_planes, (k + 1) * block_planes)
            nv_ref[c, at, :, :] = nv_ref[c, at, :, :] - column

    halo_wait(halo_recv, -1, (-1, 1))
    for k, y in ((1, 0), (2, rows - 1)):
        for edge, at in ((0, 0), (planes + 1, 3)):
            xc[k, :, at, :] = w[:, edge, y, :]
    for k in range(4):
        for edge, at in ((1, 1), (planes, 2)):
            xc[k, :, at, :] = xr[k, :, edge, :]

    lower = (d > 0).astype(F32)
    upper = (d < dom_count - 1).astype(F32)
    ahead = element_plane(planes, inside_yz * upper)
    behind = element_plane(0, inside_yz * lower)
    pair = iota((8, nz), 0)
    ends = jnp.where(pair == 0, lower, 0.0) + jnp.where(pair == 2, upper, 0.0)
    ends = jnp.where(iota((8, nz), 1) <= nz - 2, ends, 0.0)
    corners = [
        mapped(
            edge_ref.at[2 * k],
            element_blocks(
                lambda f, a, b: xc[2 * k + b, f, a : a + 8, :], xc[2 * k, 6, 0:8, :], ends * present.astype(F32)
            ),
        )[0]
        for k, y, present in sides
    ]
    for force, a, x in ((ahead, 0, planes - 1), (behind, 1, 0)):
        for m in range(3):
            for t in range(row_blocks):
                internal = part_of(force[t], m, a, 0) + pltpu.roll(part_of(force[t], m, a, 1), 1, 1)
                at = slice(8 * t, 8 * t + 8)
                nv_ref[m, x, at, :] = nv_ref[m, x, at, :] - step * internal
    for (k, y, present), force in zip(sides, corners):
        for m in range(3):
            at = m * 16
            internal = step * (force[at : at + 8, :] + pltpu.roll(force[at + 8 : at + 16, :], 1, 1))
            for j, x in ((0, 0), (1, planes - 1)):
                nv_ref[m, x, y : y + 1, :] = nv_ref[m, x, y : y + 1, :] - internal[j : j + 1, :]

    waits["nodes_sent"].wait()
    waits["tables_sent"].wait()
    halo_wait(halo_send, 1, (-1, 0, 1))


def store_kernel(nv_ref, react_ref, nv_out, react_out, sem):
    copies = [
        pltpu.make_async_copy(a, b, sem.at[i]) for i, (a, b) in enumerate(((nv_ref, nv_out), (react_ref, react_out)))
    ]
    for copy in copies:
        copy.start()
    for copy in copies:
        copy.wait()


def local(
    dom_count, sub_count, displacement, velocity, modulus, element_stiffness, viscosity, step_size, seg_tilt,
    seg_offset, seg_stiffness, projection, contact_flag, candidates,
):
    _, planes, rows, nz = displacement.shape
    seg_local = seg_offset.shape[0]
    seg_blocks = seg_local // BLK
    node_blocks = projection.shape[0]
    group_rows = node_blocks * sub_count
    vmem = pl.BlockSpec(memory_space=pltpu.VMEM)
    hbm = pl.BlockSpec(memory_space=pl.ANY)
    dma = pltpu.SemaphoreType.DMA
    results = pl.pallas_call(
        functools.partial(kernel, dom_count, sub_count),
        out_shape=(
            pltpu.VMEM(velocity.shape, F32),
            pltpu.VMEM((3, seg_local), F32),
        ),
        in_specs=[hbm] * 12,
        out_specs=(vmem, vmem),
        scratch_shapes=[
            pltpu.SMEM((1,), F32),
            pltpu.SMEM((1,), F32),
            pltpu.VMEM(candidates.shape, jnp.int32),
            pltpu.VMEM(element_stiffness.shape, BF16),
            pltpu.VMEM(seg_tilt.shape, F32),
            pltpu.VMEM(projection.shape, jnp.int32),
            pltpu.VMEM(contact_flag.shape, jnp.int32),
            pltpu.VMEM((7, planes + 2, rows + 8, nz), F32),
            pltpu.VMEM((4, 7, planes + 16, nz), F32),
            pltpu.VMEM((4, 7, 16, nz), F32),
            pltpu.VMEM((4, node_blocks, BLK), F32),
            pltpu.VMEM((4, group_rows, BLK), F32),
            pltpu.VMEM((sub_count, 4 * seg_blocks, BLK), F32),
            pltpu.VMEM((4, group_rows, BLK), F32),
            pltpu.VMEM((4, node_blocks, BLK), F32),
            pltpu.VMEM((96, 192), BF16),
            pltpu.VMEM((96, 192), BF16),
            pltpu.VMEM((4, 48, 192), BF16),
            pltpu.VMEM((6, rows // 8, 8, nz), F32),
            dma((11,)),
            dma((3,)),
            dma((3,)),
            dma((4,)),
        ],
        compiler_params=pltpu.CompilerParams(collective_id=0, has_side_effects=True),
    )(
        viscosity.reshape(1),
        step_size.reshape(1),
        candidates,
        element_stiffness,
        seg_tilt,
        seg_offset.reshape(seg_blocks, BLK),
        seg_stiffness.reshape(seg_blocks, BLK),
        projection,
        contact_flag,
        displacement,
        velocity,
        modulus,
    )
    return pl.pallas_call(
        store_kernel,
        out_shape=tuple(jax.ShapeDtypeStruct(x.shape, F32) for x in results),
        in_specs=[vmem, vmem],
        out_specs=(hbm, hbm),
        scratch_shapes=[dma((2,))],
    )(*(pltpu.with_memory_space_constraint(x, pltpu.VMEM) for x in results))


def solution(mesh):
    return jax.shard_map(
        functools.partial(local, mesh.shape["dom"], mesh.shape["sub"]),
        mesh=mesh,
        in_specs=(
            P(None, "dom", "sub", None),
            P(None, "dom", "sub", None),
            P("dom", "sub", None),
            P(),
            P(),
            P(),
            P(None, ("dom", "sub")),
            P(("dom", "sub")),
            P(("dom", "sub")),
            P(("dom", "sub"), None),
            P(("dom", "sub"), None),
            P(("dom", "sub"), None),
        ),
        out_specs=(P(None, "dom", "sub", None), P(None, ("dom", "sub"))),
        check_vma=False,
    )
```

```python
import functools

import jax
import jax.numpy as jnp
from jax import lax
from jax.experimental import pallas as pl
from jax.experimental.pallas import tpu as pltpu
from jax.sharding import PartitionSpec as P

MESH = pl.DeviceIdType.MESH
BLK = 128
UNROLL = 3
F32 = jnp.float32
BF16 = jnp.bfloat16
DIRS = tuple((dx, dy) for dx in (-1, 0, 1) for dy in (-1, 0, 1) if (dx, dy) != (0, 0))


def iota(shape, axis):
    return lax.broadcasted_iota(jnp.int32, shape, axis)


def split3(x):
    hi = x.astype(BF16)
    rest = x - hi.astype(F32)
    mid = rest.astype(BF16)
    low = (rest - mid.astype(F32)).astype(BF16)
    return hi, mid, low


def stiffness_maps(stiff):
    row = iota((96, 24), 0) // 8
    col = iota((96, 24), 1)
    wide = (iota((24, 192), 0) == iota((24, 192), 1) // 8).astype(BF16)
    parts = []
    for corner_y in (0, 1):
        pick = (col == (row // 2) * 4 + row % 2 + 2 * corner_y).astype(BF16)
        rows = jnp.dot(pick, stiff, preferred_element_type=F32).astype(BF16)
        parts.append(jnp.dot(rows, wide, preferred_element_type=F32))
    to_y = iota((96, 192), 0) % 8
    from_y = iota((96, 192), 1) % 8
    same = jnp.where(from_y == to_y, parts[0], 0.0) + jnp.where(from_y + 1 == to_y, parts[1], 0.0)
    carry = jnp.where((from_y == 7) & (to_y == 0), parts[1], 0.0)
    return same.astype(BF16), carry.astype(BF16)


def edge_maps(stiff, corner_y):
    row = iota((48, 24), 0) // 8
    col = iota((48, 24), 1)
    wide = (iota((24, 192), 0) == iota((24, 192), 1) // 8).astype(BF16)
    parts = []
    for corner_x in (0, 1):
        pick = (col == (row // 2) * 8 + row % 2 + 4 * corner_x + 2 * corner_y).astype(BF16)
        rows = jnp.dot(pick, stiff, preferred_element_type=F32).astype(BF16)
        parts.append(jnp.dot(rows, wide, preferred_element_type=F32))
    to_x = iota((48, 192), 0) % 8
    from_x = iota((48, 192), 1) % 8
    same = jnp.where(from_x == to_x, parts[1], 0.0) + jnp.where(from_x == to_x + 1, parts[0], 0.0)
    following = jnp.where((from_x == 0) & (to_x == 7), parts[0], 0.0)
    return same.astype(BF16), following.astype(BF16)


def kernel(
    dom_count, sub_count, visc_hbm, step_hbm, cand_hbm, stiff_hbm, tilt_hbm, off_hbm, stf_hbm, proj_hbm, flag_hbm,
    disp, vel, mod, nv_ref, react_ref, visc_ref, step_ref, cand_ref, stiff_ref, tilt_ref, proj_ref, flag_ref,
    w, xr, xc, msg, nodes, tables, values, own_values, same_ref, carry_ref, edge_ref, prev,
    local_sem, halo_send, halo_recv, peer_sem,
):
    d = lax.axis_index("dom")
    s = lax.axis_index("sub")
    planes, rows, nz = disp.shape[1], disp.shape[2], disp.shape[3]
    inner = slice(1, 1 + planes)
    table = tables.at[0]
    seg_blocks = off_hbm.shape[0]
    node_blocks = proj_ref.shape[0]
    def exists(dx, dy):
        cond = (d + dx >= 0) & (d + dx < dom_count)
        return cond & (s + dy >= 0) & (s + dy < sub_count)

    xc[...] = jnp.zeros(xc.shape, F32)
    barrier = pltpu.get_barrier_semaphore()
    for off in range(1, sub_count):
        pl.semaphore_signal(barrier, inc=1, device_id=(d, (s + off) % sub_count), device_id_type=MESH)
    for dx, dy in DIRS:
        if dx != 0:

            @pl.when(exists(dx, dy))
            def _():
                pl.semaphore_signal(barrier, inc=1, device_id=(d + dx, s + dy), device_id_type=MESH)

    own = w.at[:, inner, 0:rows, :]
    stages = (
        ("stiff", ((stiff_hbm, stiff_ref),), stiff_ref),
        ("proj", ((proj_hbm, proj_ref),), proj_ref),
        ("flag", ((flag_hbm, flag_ref),), flag_ref),
        ("cand", ((cand_hbm, cand_ref),), cand_ref),
        ("disp", ((disp, own.at[0:3]),), own.at[0:3]),
        ("vel", ((vel, own.at[3:6]), (mod, own.at[6])), own.at[3:7]),
        ("tilt", ((tilt_hbm, tilt_ref),), tilt_ref),
        (
            "table",
            (
                (off_hbm, table.at[2 * seg_blocks : 3 * seg_blocks, :]),
                (stf_hbm, table.at[3 * seg_blocks : 4 * seg_blocks, :]),
            ),
            table.at[2 * seg_blocks : 4 * seg_blocks, :],
        ),
        ("visc", ((visc_hbm, visc_ref),), visc_ref),
        ("step", ((step_hbm, step_ref),), step_ref),
        (
            "rows",
            tuple(
                copy
                for k, y in ((1, 0), (2, rows - 1))
                for copy in (
                    (disp.at[:, :, y, :], xr.at[k, 0:3, inner, :]),
                    (vel.at[:, :, y, :], xr.at[k, 3:6, inner, :]),
                    (mod.at[:, y, :], xr.at[k, 6, inner, :]),
                )
            ),
            xr.at[1:3, :, inner, :],
        ),
    )
    waits = {}
    for i, (name, pairs, whole) in enumerate(stages):
        for a, b in pairs:
            pltpu.make_async_copy(a, b, local_sem.at[i]).start()
        waits[name] = pltpu.make_async_copy(whole, whole, local_sem.at[i])

    w[:, :, rows : rows + 8, :] = jnp.zeros((7, planes + 2, 8, nz), F32)
    for k in (0, 1, 2, 3):
        xr[k, :, 0:1, :] = jnp.zeros((7, 1, nz), F32)
        xr[k, :, planes + 1 :, :] = jnp.zeros((7, xr.shape[2] - planes - 1, nz), F32)
    for dx, edge in ((1, 0), (-1, planes + 1)):

        @pl.when(jnp.logical_not(exists(-dx, 0)))
        def _():
            w[:, edge, 0:rows, :] = jnp.zeros((7, rows, nz), F32)

    for dy, k in ((1, 0), (-1, 3)):

        @pl.when(jnp.logical_not(exists(0, -dy)))
        def _():
            xr[k, :, 1 : planes + 1, :] = jnp.zeros((7, planes, nz), F32)

    waits["stiff"].wait()
    same, carry = stiffness_maps(stiff_ref[...])
    same_ref[...] = same
    carry_ref[...] = carry
    for k in (0, 1):
        same, following = edge_maps(stiff_ref[...], 1 - k)
        edge_ref[2 * k] = same
        edge_ref[2 * k + 1] = following

    for name in ("proj", "flag", "cand", "disp"):
        waits[name].wait()
    block_planes = BLK // rows
    group_start = d * (seg_blocks * BLK * sub_count)
    target = proj_ref[...] - group_start
    target_block = target // BLK
    listed = jnp.zeros(target.shape, jnp.bool_)
    for slot in range(cand_ref.shape[1]):
        listed = listed | (target_block == cand_ref[:, slot : slot + 1])
    chosen = jnp.where(listed & (flag_ref[...] == 1), target, -1).astype(F32)
    for c in range(3):
        for k in range(node_blocks):
            part = w[c, 1 + k * block_planes : 1 + (k + 1) * block_planes, 0:rows, :].reshape(BLK, nz)
            msg[c, k : k + 1, :] = jnp.transpose(part)[nz - 1 : nz, :]
    msg[3] = chosen

    for name in ("tilt", "table", "visc", "step"):
        waits[name].wait()
    for b in range(seg_blocks):
        lanes = slice(b * BLK, (b + 1) * BLK)
        for c in range(2):
            table[c * seg_blocks + b : c * seg_blocks + b + 1, :] = tilt_ref[c : c + 1, lanes]
    columns = 1 + (s > 0).astype(jnp.int32) + (s < sub_count - 1).astype(jnp.int32)
    sides = (d > 0).astype(jnp.int32) + (d < dom_count - 1).astype(jnp.int32)
    pl.semaphore_wait(barrier, sub_count - 1 + columns * sides)

    waits["vel"].wait()

    def halo_copy(dx, dy):
        src_x = {1: planes, -1: 1, 0: inner}[dx]
        dst_x = {1: 0, -1: planes + 1, 0: inner}[dx]
        if dy == 0:
            a, b = w.at[:, src_x, 0:rows, :], w.at[:, dst_x, 0:rows, :]
        else:
            k = 0 if dy > 0 else 3
            a = w.at[:, src_x, rows - 1 if dy > 0 else 0, :]
            b = xr.at[k, :, inner, :] if dx == 0 else xc.at[k, :, 0 if dx > 0 else 3, :]
        return pltpu.make_async_remote_copy(
            src_ref=a,
            dst_ref=b,
            send_sem=halo_send.at[dx + 1],
            recv_sem=halo_recv.at[dx + 1],
            device_id=(d + dx, s + dy),
            device_id_type=MESH,
        )

    def send_halo(dirs):
        for dx, dy in dirs:

            @pl.when(exists(dx, dy))
            def _():
                halo_copy(dx, dy).start()

    send_halo([(dx, dy) for dx, dy in DIRS if dy == 0])

    def node_copy(off):
        return pltpu.make_async_remote_copy(
            src_ref=msg,
            dst_ref=nodes.at[:, node_blocks * off : node_blocks * (off + 1), :],
            send_sem=peer_sem.at[0],
            recv_sem=peer_sem.at[1],
            device_id=(d, (s + off) % sub_count),
            device_id_type=MESH,
        )

    for off in range(1, sub_count):
        node_copy(off).start()
    def table_copy(off):
        return pltpu.make_async_remote_copy(
            src_ref=table,
            dst_ref=tables.at[off],
            send_sem=peer_sem.at[2],
            recv_sem=peer_sem.at[3],
            device_id=(d, (s + off) % sub_count),
            device_id_type=MESH,
        )

    for off in range(1, sub_count):
        table_copy(off).start()
    send_halo([(dx, dy) for dx, dy in DIRS if dy != 0])
    received = tables.at[1:sub_count]
    waits["tables_sent"] = pltpu.make_async_copy(received, received, peer_sem.at[2])
    waits["tables"] = pltpu.make_async_copy(received, received, peer_sem.at[3])
    nodes_all = nodes.at[:, node_blocks : node_blocks * sub_count, :]
    waits["nodes_sent"] = pltpu.make_async_copy(nodes_all, nodes_all, peer_sem.at[0])
    waits["nodes"] = pltpu.make_async_copy(nodes_all, nodes_all, peer_sem.at[1])
    def halo_wait(sem, sign, sides):
        both = (s > 0) & (s < sub_count - 1)
        for dx in sides:
            for many, present in ((2, both), (1, jnp.logical_not(both))):
                if dx == 0:
                    part = w.at[:, 0:planes, 0:many, :]
                else:
                    part = w.at[:, 0 : rows + many, 0, :]

                @pl.when(present & exists(sign * dx, 0))
                def _():
                    pltpu.make_async_copy(part, part, sem.at[dx + 1]).wait()

    nodes[:, 0:node_blocks, :] = msg[...]
    viscosity = visc_ref[0]
    step = step_ref[0]
    row_blocks = rows // 8

    def element_blocks(view, modulus, mask):
        def corner_views(field, a):
            flat = [view(field, a, b) for b in (0, 1)]
            return [[x, pltpu.roll(x, nz - 1, 1)] for x in flat]

        speed = [[corner_views(3 + m, a) for a in (0, 1)] for m in range(3)]
        rate = None
        for m in range(3):
            for a in (0, 1):
                for b in (0, 1):
                    for c in (0, 1):
                        term = speed[m][a][b][c]
                        sign = (a, b, c)[m]
                        if rate is None:
                            rate = -term
                        else:
                            rate = rate + term if sign else rate - term
        bulk = (viscosity * mask) * jnp.maximum(-0.25 * rate, 0.0)
        factor = mask * modulus
        entries = []
        for m in range(3):
            for a in (0, 1):
                disps = corner_views(m, a)
                for b in (0, 1):
                    for c in (0, 1):
                        entries.append(factor * disps[b][c] + bulk * speed[m][a][b][c])
        return [
            jnp.concatenate([x[8 * t : 8 * t + 8, :] for x in entries], axis=0).astype(BF16)
            for t in range(entries[0].shape[0] // 8)
        ]

    def mapped(map_ref, blocks):
        wide = jnp.dot(map_ref[...], jnp.concatenate(blocks, axis=1), preferred_element_type=F32)
        return [wide[:, t * nz : (t + 1) * nz] for t in range(len(blocks))]

    inside_yz = ((iota((rows, nz), 0) <= rows - 2) & (iota((rows, nz), 1) <= nz - 2)).astype(F32)

    def element_plane(e, mask):
        blocks = element_blocks(lambda f, a, b: w[f, e + a, b : b + rows, :], w[6, e, 0:rows, :], mask)
        force = mapped(same_ref, blocks)
        carried = mapped(carry_ref, blocks[:-1]) if row_blocks > 1 else []
        return [force[0]] + [x + y for x, y in zip(force[1:], carried)]

    def part_of(force, m, a, c):
        at = ((m * 2 + a) * 2 + c) * 8
        return force[at : at + 8, :]

    def node_plane(e, force):
        for m in range(3):
            for t in range(row_blocks):
                part = [part_of(force[t], m, 0, c) + prev[m * 2 + c, t] for c in (0, 1)]
                internal = part[0] + pltpu.roll(part[1], 1, 1)
                at = slice(8 * t, 8 * t + 8)
                nv_ref[m, e - 1, at, :] = w[3 + m, e, at, :] - step * internal

    def advance(e):
        force = element_plane(e, inside_yz)
        node_plane(e, force)
        for m in range(3):
            for c in (0, 1):
                for t in range(row_blocks):
                    prev[m * 2 + c, t] = part_of(force[t], m, 1, c)

    prev[...] = jnp.zeros(prev.shape, F32)
    group = UNROLL if (planes - 1) % UNROLL == 0 else 1

    def advance_group(g):
        for i in range(group):
            advance(1 + g * group + i)

    @pl.loop(0, (planes - 1) // group)
    def _(g):
        advance_group(g)

    for m in range(3):
        for t in range(row_blocks):
            internal = prev[m * 2, t] + pltpu.roll(prev[m * 2 + 1, t], 1, 1)
            at = slice(8 * t, 8 * t + 8)
            nv_ref[m, planes - 1, at, :] = w[3 + m, planes, at, :] - step * internal

    lane_rows = iota((BLK, BLK), 0)

    def one_hot(lane):
        return jnp.concatenate(
            [(lane_rows == lane[r : r + 1, :]).astype(F32).astype(BF16) for r in range(lane.shape[0])], axis=1
        )

    own_valid = msg[3] >= 0.0
    own_wanted = jnp.where(own_valid, msg[3].astype(jnp.int32), 0)
    slot = (s + sub_count - own_wanted // (seg_blocks * BLK)) % sub_count
    own_block = slot * seg_blocks + own_wanted % (seg_blocks * BLK) // BLK
    own_block = jnp.where(own_valid, own_block, -1)
    own_hot = one_hot(own_wanted % BLK)
    own_rows = iota((sub_count * seg_blocks, BLK), 0)
    own_in_block = [own_rows == own_block[r : r + 1, :] for r in range(node_blocks)]
    own_parts = jnp.concatenate(split3(table[...]), axis=0)

    waits["nodes"].wait()

    group_rows = node_blocks * sub_count
    def contact(slots, parts, store, hot, in_block, valid, place):
        found = jnp.dot(parts, hot, preferred_element_type=F32)
        count = slots * 4 * seg_blocks
        found = found[0:count] + found[count : 2 * count] + found[2 * count : 3 * count]
        for f in range(4):
            for r in range(len(in_block)):
                picked = None
                for k in range(slots):
                    at = (k * 4 + f) * seg_blocks
                    field = found[at : at + seg_blocks, r * BLK : (r + 1) * BLK]
                    term = jnp.where(in_block[r][k * seg_blocks : (k + 1) * seg_blocks], field, 0.0)
                    picked = term if picked is None else picked + term
                store[f, r : r + 1, :] = jnp.sum(picked, axis=0, keepdims=True)
        tilt_x, tilt_y = store[0], store[1]
        unit = 1.0 / jnp.sqrt(1.0 + tilt_x * tilt_x + tilt_y * tilt_y)
        normal = (tilt_x * unit, tilt_y * unit, unit)
        depth = normal[0] * place[0] + normal[1] * place[1] + normal[2] * place[2] - store[2]
        pressure = jnp.where(valid, store[3] * jnp.maximum(depth, 0.0), 0.0)
        return [pressure * n for n in normal]

    wanted = nodes[3].astype(jnp.int32) - s * (seg_blocks * BLK)
    valid = (nodes[3] >= 0.0) & (wanted >= 0) & (wanted < seg_blocks * BLK)
    wanted = jnp.where(valid, wanted, 0)
    block = jnp.where(valid, wanted // BLK, -1)
    hot = one_hot(wanted % BLK)
    block_rows = iota((seg_blocks, BLK), 0)
    in_block = [block_rows == block[r : r + 1, :] for r in range(group_rows)]
    loads = contact(1, own_parts, values, hot, in_block, valid, nodes)
    spread = jnp.concatenate(
        [
            jnp.concatenate([jnp.where(in_block[r], loads[c][r : r + 1, :], 0.0) for r in range(group_rows)], axis=1)
            for c in range(3)
        ],
        axis=0,
    )
    high = spread.astype(BF16)
    low = (spread - high.astype(F32)).astype(BF16)
    summed = lax.dot_general(
        jnp.concatenate([high, low], axis=0), hot, (((1,), (1,)), ((), ())), preferred_element_type=F32
    )
    summed = summed[0 : 3 * seg_blocks] + summed[3 * seg_blocks :]
    for c in range(3):
        for b in range(seg_blocks):
            at = c * seg_blocks + b
            react_ref[c : c + 1, b * BLK : (b + 1) * BLK] = summed[at : at + 1, :]

    waits["tables"].wait()
    parts = jnp.concatenate(split3(tables[...].reshape(sub_count * 4 * seg_blocks, BLK)), axis=0)
    loads = contact(sub_count, parts, own_values, own_hot, own_in_block, own_valid, msg)
    top = iota((nz, BLK), 0) == nz - 1
    for c in range(3):
        total = step * loads[c]
        for k in range(node_blocks):
            column = jnp.transpose(jnp.where(top, total[k : k + 1, :], 0.0)).reshape(block_planes, rows, nz)
            at = slice(k * block_planes, (k + 1) * block_planes)
            nv_ref[c, at, :, :] = nv_ref[c, at, :, :] - column

    waits["rows"].wait()
    halo_wait(halo_recv, -1, (0,))
    sides = ((0, 0, s > 0), (1, rows - 1, s < sub_count - 1))
    along = iota((planes, nz), 0)
    inside_xz = ((along >= 1) & (iota((planes, nz), 1) <= nz - 2)).astype(F32)
    for k, y, present in sides:
        blocks = element_blocks(
            lambda f, a, b: xr[2 * k + b, f, a : a + planes, :],
            xr[2 * k, 6, 0:planes, :],
            inside_xz * present.astype(F32),
        )
        here = mapped(edge_ref.at[2 * k], blocks)
        after = mapped(edge_ref.at[2 * k + 1], blocks[1:]) if planes > 8 else []
        for t in range(planes // 8):
            force = here[t] + after[t] if t < len(after) else here[t]
            for m in range(3):
                at = m * 16
                internal = step * (force[at : at + 8, :] + pltpu.roll(force[at + 8 : at + 16, :], 1, 1))
                for j in range(8):
                    x = 8 * t + j
                    nv_ref[m, x, y : y + 1, :] = nv_ref[m, x, y : y + 1, :] - internal[j : j + 1, :]

    halo_wait(halo_recv, -1, (-1, 1))
    for k, y in ((1, 0), (2, rows - 1)):
        for edge, at in ((0, 0), (planes + 1, 3)):
            xc[k, :, at, :] = w[:, edge, y, :]
    for k in range(4):
        for edge, at in ((1, 1), (planes, 2)):
            xc[k, :, at, :] = xr[k, :, edge, :]

    lower = (d > 0).astype(F32)
    upper = (d < dom_count - 1).astype(F32)
    ahead = element_plane(planes, inside_yz * upper)
    behind = element_plane(0, inside_yz * lower)
    pair = iota((8, nz), 0)
    ends = jnp.where(pair == 0, lower, 0.0) + jnp.where(pair == 2, upper, 0.0)
    ends = jnp.where(iota((8, nz), 1) <= nz - 2, ends, 0.0)
    corners = [
        mapped(
            edge_ref.at[2 * k],
            element_blocks(
                lambda f, a, b: xc[2 * k + b, f, a : a + 8, :], xc[2 * k, 6, 0:8, :], ends * present.astype(F32)
            ),
        )[0]
        for k, y, present in sides
    ]
    for force, a, x in ((ahead, 0, planes - 1), (behind, 1, 0)):
        for m in range(3):
            for t in range(row_blocks):
                internal = part_of(force[t], m, a, 0) + pltpu.roll(part_of(force[t], m, a, 1), 1, 1)
                at = slice(8 * t, 8 * t + 8)
                nv_ref[m, x, at, :] = nv_ref[m, x, at, :] - step * internal
    for (k, y, present), force in zip(sides, corners):
        for m in range(3):
            at = m * 16
            internal = step * (force[at : at + 8, :] + pltpu.roll(force[at + 8 : at + 16, :], 1, 1))
            for j, x in ((0, 0), (1, planes - 1)):
                nv_ref[m, x, y : y + 1, :] = nv_ref[m, x, y : y + 1, :] - internal[j : j + 1, :]

    waits["nodes_sent"].wait()
    waits["tables_sent"].wait()
    halo_wait(halo_send, 1, (-1, 0, 1))


def store_kernel(nv_ref, react_ref, nv_out, react_out, sem):
    copies = [
        pltpu.make_async_copy(a, b, sem.at[i]) for i, (a, b) in enumerate(((nv_ref, nv_out), (react_ref, react_out)))
    ]
    for copy in copies:
        copy.start()
    for copy in copies:
        copy.wait()


def local(
    dom_count, sub_count, displacement, velocity, modulus, element_stiffness, viscosity, step_size, seg_tilt,
    seg_offset, seg_stiffness, projection, contact_flag, candidates,
):
    _, planes, rows, nz = displacement.shape
    seg_local = seg_offset.shape[0]
    seg_blocks = seg_local // BLK
    node_blocks = projection.shape[0]
    group_rows = node_blocks * sub_count
    vmem = pl.BlockSpec(memory_space=pltpu.VMEM)
    hbm = pl.BlockSpec(memory_space=pl.ANY)
    dma = pltpu.SemaphoreType.DMA
    results = pl.pallas_call(
        functools.partial(kernel, dom_count, sub_count),
        out_shape=(
            pltpu.VMEM(velocity.shape, F32),
            pltpu.VMEM((3, seg_local), F32),
        ),
        in_specs=[hbm] * 12,
        out_specs=(vmem, vmem),
        scratch_shapes=[
            pltpu.SMEM((1,), F32),
            pltpu.SMEM((1,), F32),
            pltpu.VMEM(candidates.shape, jnp.int32),
            pltpu.VMEM(element_stiffness.shape, BF16),
            pltpu.VMEM(seg_tilt.shape, F32),
            pltpu.VMEM(projection.shape, jnp.int32),
            pltpu.VMEM(contact_flag.shape, jnp.int32),
            pltpu.VMEM((7, planes + 2, rows + 8, nz), F32),
            pltpu.VMEM((4, 7, planes + 16, nz), F32),
            pltpu.VMEM((4, 7, 16, nz), F32),
            pltpu.VMEM((4, node_blocks, BLK), F32),
            pltpu.VMEM((4, group_rows, BLK), F32),
            pltpu.VMEM((sub_count, 4 * seg_blocks, BLK), F32),
            pltpu.VMEM((4, group_rows, BLK), F32),
            pltpu.VMEM((4, node_blocks, BLK), F32),
            pltpu.VMEM((96, 192), BF16),
            pltpu.VMEM((96, 192), BF16),
            pltpu.VMEM((4, 48, 192), BF16),
            pltpu.VMEM((6, rows // 8, 8, nz), F32),
            dma((11,)),
            dma((3,)),
            dma((3,)),
            dma((4,)),
        ],
        compiler_params=pltpu.CompilerParams(collective_id=0, has_side_effects=True),
    )(
        viscosity.reshape(1),
        step_size.reshape(1),
        candidates,
        element_stiffness,
        seg_tilt,
        seg_offset.reshape(seg_blocks, BLK),
        seg_stiffness.reshape(seg_blocks, BLK),
        projection,
        contact_flag,
        displacement,
        velocity,
        modulus,
    )
    return pl.pallas_call(
        store_kernel,
        out_shape=tuple(jax.ShapeDtypeStruct(x.shape, F32) for x in results),
        in_specs=[vmem, vmem],
        out_specs=(hbm, hbm),
        scratch_shapes=[dma((2,))],
    )(*(pltpu.with_memory_space_constraint(x, pltpu.VMEM) for x in results))


def solution(mesh):
    return jax.shard_map(
        functools.partial(local, mesh.shape["dom"], mesh.shape["sub"]),
        mesh=mesh,
        in_specs=(
            P(None, "dom", "sub", None),
            P(None, "dom", "sub", None),
            P("dom", "sub", None),
            P(),
            P(),
            P(),
            P(None, ("dom", "sub")),
            P(("dom", "sub")),
            P(("dom", "sub")),
            P(("dom", "sub"), None),
            P(("dom", "sub"), None),
            P(("dom", "sub"), None),
        ),
        out_specs=(P(None, "dom", "sub", None), P(None, ("dom", "sub"))),
        check_vma=False,
    )
```

```python
import functools

import jax
import jax.numpy as jnp
from jax import lax
from jax.experimental import pallas as pl
from jax.experimental.pallas import tpu as pltpu
from jax.sharding import PartitionSpec as P

MESH = pl.DeviceIdType.MESH
BLK = 128
UNROLL = 3
F32 = jnp.float32
BF16 = jnp.bfloat16
DIRS = tuple((dx, dy) for dx in (-1, 0, 1) for dy in (-1, 0, 1) if (dx, dy) != (0, 0))


def iota(shape, axis):
    return lax.broadcasted_iota(jnp.int32, shape, axis)


def split3(x):
    hi = x.astype(BF16)
    rest = x - hi.astype(F32)
    mid = rest.astype(BF16)
    low = (rest - mid.astype(F32)).astype(BF16)
    return hi, mid, low


def stiffness_maps(stiff):
    row = iota((96, 24), 0) // 8
    col = iota((96, 24), 1)
    wide = (iota((24, 192), 0) == iota((24, 192), 1) // 8).astype(BF16)
    parts = []
    for corner_y in (0, 1):
        pick = (col == (row // 2) * 4 + row % 2 + 2 * corner_y).astype(BF16)
        rows = jnp.dot(pick, stiff, preferred_element_type=F32).astype(BF16)
        parts.append(jnp.dot(rows, wide, preferred_element_type=F32))
    to_y = iota((96, 192), 0) % 8
    from_y = iota((96, 192), 1) % 8
    same = jnp.where(from_y == to_y, parts[0], 0.0) + jnp.where(from_y + 1 == to_y, parts[1], 0.0)
    carry = jnp.where((from_y == 7) & (to_y == 0), parts[1], 0.0)
    return same.astype(BF16), carry.astype(BF16)


def edge_maps(stiff, corner_y):
    row = iota((48, 24), 0) // 8
    col = iota((48, 24), 1)
    wide = (iota((24, 192), 0) == iota((24, 192), 1) // 8).astype(BF16)
    parts = []
    for corner_x in (0, 1):
        pick = (col == (row // 2) * 8 + row % 2 + 4 * corner_x + 2 * corner_y).astype(BF16)
        rows = jnp.dot(pick, stiff, preferred_element_type=F32).astype(BF16)
        parts.append(jnp.dot(rows, wide, preferred_element_type=F32))
    to_x = iota((48, 192), 0) % 8
    from_x = iota((48, 192), 1) % 8
    same = jnp.where(from_x == to_x, parts[1], 0.0) + jnp.where(from_x == to_x + 1, parts[0], 0.0)
    following = jnp.where((from_x == 0) & (to_x == 7), parts[0], 0.0)
    return same.astype(BF16), following.astype(BF16)


def kernel(
    dom_count, sub_count, visc_hbm, step_hbm, cand_hbm, stiff_hbm, tilt_hbm, off_hbm, stf_hbm, proj_hbm, flag_hbm,
    disp, vel, mod, nv_ref, react_ref, visc_ref, step_ref, cand_ref, stiff_ref, tilt_ref, proj_ref, flag_ref,
    w, xr, xc, msg, nodes, tables, values, own_values, same_ref, carry_ref, edge_ref, prev,
    local_sem, halo_send, halo_recv, peer_sem,
):
    d = lax.axis_index("dom")
    s = lax.axis_index("sub")
    planes, rows, nz = disp.shape[1], disp.shape[2], disp.shape[3]
    inner = slice(1, 1 + planes)
    table = tables.at[0]
    seg_blocks = off_hbm.shape[0]
    node_blocks = proj_ref.shape[0]
    def exists(dx, dy):
        cond = (d + dx >= 0) & (d + dx < dom_count)
        return cond & (s + dy >= 0) & (s + dy < sub_count)

    xc[...] = jnp.zeros(xc.shape, F32)
    barrier = pltpu.get_barrier_semaphore()
    for off in range(1, sub_count):
        pl.semaphore_signal(barrier, inc=1, device_id=(d, (s + off) % sub_count), device_id_type=MESH)
    for dx, dy in DIRS:
        if dx != 0:

            @pl.when(exists(dx, dy))
            def _():
                pl.semaphore_signal(barrier, inc=1, device_id=(d + dx, s + dy), device_id_type=MESH)

    own = w.at[:, inner, 0:rows, :]
    stages = (
        ("stiff", ((stiff_hbm, stiff_ref),), stiff_ref),
        ("proj", ((proj_hbm, proj_ref),), proj_ref),
        ("flag", ((flag_hbm, flag_ref),), flag_ref),
        ("cand", ((cand_hbm, cand_ref),), cand_ref),
        ("disp", ((disp, own.at[0:3]),), own.at[0:3]),
        ("vel", ((vel, own.at[3:6]), (mod, own.at[6])), own.at[3:7]),
        ("tilt", ((tilt_hbm, tilt_ref),), tilt_ref),
        (
            "table",
            (
                (off_hbm, table.at[2 * seg_blocks : 3 * seg_blocks, :]),
                (stf_hbm, table.at[3 * seg_blocks : 4 * seg_blocks, :]),
            ),
            table.at[2 * seg_blocks : 4 * seg_blocks, :],
        ),
        ("visc", ((visc_hbm, visc_ref),), visc_ref),
        ("step", ((step_hbm, step_ref),), step_ref),
        (
            "rows",
            tuple(
                copy
                for k, y in ((1, 0), (2, rows - 1))
                for copy in (
                    (disp.at[:, :, y, :], xr.at[k, 0:3, inner, :]),
                    (vel.at[:, :, y, :], xr.at[k, 3:6, inner, :]),
                    (mod.at[:, y, :], xr.at[k, 6, inner, :]),
                )
            ),
            xr.at[1:3, :, inner, :],
        ),
    )
    waits = {}
    for i, (name, pairs, whole) in enumerate(stages):
        for a, b in pairs:
            pltpu.make_async_copy(a, b, local_sem.at[i]).start()
        waits[name] = pltpu.make_async_copy(whole, whole, local_sem.at[i])

    w[:, :, rows : rows + 8, :] = jnp.zeros((7, planes + 2, 8, nz), F32)
    w[6, planes + 1, 0:rows, :] = jnp.zeros((rows, nz), F32)
    for k in (0, 1, 2, 3):
        xr[k, :, 0:1, :] = jnp.zeros((7, 1, nz), F32)
        xr[k, :, planes + 1 :, :] = jnp.zeros((7, xr.shape[2] - planes - 1, nz), F32)
    for dx, edge in ((1, 0), (-1, planes + 1)):

        @pl.when(jnp.logical_not(exists(-dx, 0)))
        def _():
            w[0:6, edge, 0:rows, :] = jnp.zeros((6, rows, nz), F32)
            if dx > 0:
                w[6, edge, 0:rows, :] = jnp.zeros((rows, nz), F32)

    for dy, k in ((1, 0), (-1, 3)):

        @pl.when(jnp.logical_not(exists(0, -dy)))
        def _():
            xr[k, :, 1 : planes + 1, :] = jnp.zeros((7, planes, nz), F32)

    waits["stiff"].wait()
    same, carry = stiffness_maps(stiff_ref[...])
    same_ref[...] = same
    carry_ref[...] = carry
    for k in (0, 1):
        same, following = edge_maps(stiff_ref[...], 1 - k)
        edge_ref[2 * k] = same
        edge_ref[2 * k + 1] = following

    for name in ("proj", "flag", "cand", "disp"):
        waits[name].wait()
    block_planes = BLK // rows
    group_start = d * (seg_blocks * BLK * sub_count)
    target = proj_ref[...] - group_start
    target_block = target // BLK
    listed = jnp.zeros(target.shape, jnp.bool_)
    for slot in range(cand_ref.shape[1]):
        listed = listed | (target_block == cand_ref[:, slot : slot + 1])
    chosen = jnp.where(listed & (flag_ref[...] == 1), target, -1).astype(F32)
    for c in range(3):
        for k in range(node_blocks):
            part = w[c, 1 + k * block_planes : 1 + (k + 1) * block_planes, 0:rows, :].reshape(BLK, nz)
            msg[c, k : k + 1, :] = jnp.transpose(part)[nz - 1 : nz, :]
    msg[3] = chosen

    for name in ("tilt", "table", "visc", "step"):
        waits[name].wait()
    for b in range(seg_blocks):
        lanes = slice(b * BLK, (b + 1) * BLK)
        for c in range(2):
            table[c * seg_blocks + b : c * seg_blocks + b + 1, :] = tilt_ref[c : c + 1, lanes]
    columns = 1 + (s > 0).astype(jnp.int32) + (s < sub_count - 1).astype(jnp.int32)
    sides = (d > 0).astype(jnp.int32) + (d < dom_count - 1).astype(jnp.int32)
    pl.semaphore_wait(barrier, sub_count - 1 + columns * sides)

    waits["vel"].wait()

    def halo_copy(dx, dy):
        src_x = {1: planes, -1: 1, 0: inner}[dx]
        dst_x = {1: 0, -1: planes + 1, 0: inner}[dx]
        fields = slice(0, 6) if dx < 0 else slice(0, 7)
        if dy == 0:
            a, b = w.at[fields, src_x, 0:rows, :], w.at[fields, dst_x, 0:rows, :]
        else:
            k = 0 if dy > 0 else 3
            a = w.at[fields, src_x, rows - 1 if dy > 0 else 0, :]
            b = xr.at[k, :, inner, :] if dx == 0 else xc.at[k, fields, 0 if dx > 0 else 3, :]
        return pltpu.make_async_remote_copy(
            src_ref=a,
            dst_ref=b,
            send_sem=halo_send.at[dx + 1],
            recv_sem=halo_recv.at[dx + 1],
            device_id=(d + dx, s + dy),
            device_id_type=MESH,
        )

    def send_halo(dirs):
        for dx, dy in dirs:

            @pl.when(exists(dx, dy))
            def _():
                halo_copy(dx, dy).start()

    send_halo([(dx, dy) for dx, dy in DIRS if dy == 0])

    def node_copy(off):
        return pltpu.make_async_remote_copy(
            src_ref=msg,
            dst_ref=nodes.at[:, node_blocks * off : node_blocks * (off + 1), :],
            send_sem=peer_sem.at[0],
            recv_sem=peer_sem.at[1],
            device_id=(d, (s + off) % sub_count),
            device_id_type=MESH,
        )

    for off in range(1, sub_count):
        node_copy(off).start()
    def table_copy(off):
        return pltpu.make_async_remote_copy(
            src_ref=table,
            dst_ref=tables.at[off],
            send_sem=peer_sem.at[2],
            recv_sem=peer_sem.at[3],
            device_id=(d, (s + off) % sub_count),
            device_id_type=MESH,
        )

    for off in range(1, sub_count):
        table_copy(off).start()
    send_halo([(dx, dy) for dx, dy in DIRS if dy != 0])
    received = tables.at[1:sub_count]
    waits["tables_sent"] = pltpu.make_async_copy(received, received, peer_sem.at[2])
    waits["tables"] = pltpu.make_async_copy(received, received, peer_sem.at[3])
    nodes_all = nodes.at[:, node_blocks : node_blocks * sub_count, :]
    waits["nodes_sent"] = pltpu.make_async_copy(nodes_all, nodes_all, peer_sem.at[0])
    waits["nodes"] = pltpu.make_async_copy(nodes_all, nodes_all, peer_sem.at[1])
    def halo_wait(sem, sign, sides):
        both = (s > 0) & (s < sub_count - 1)
        for dx in sides:
            for many, present in ((2, both), (1, jnp.logical_not(both))):
                if dx == 0:
                    part = w.at[:, 0:planes, 0:many, :]
                else:
                    part = w.at[0 : 6 if dx < 0 else 7, 0 : rows + many, 0, :]

                @pl.when(present & exists(sign * dx, 0))
                def _():
                    pltpu.make_async_copy(part, part, sem.at[dx + 1]).wait()

    nodes[:, 0:node_blocks, :] = msg[...]
    viscosity = visc_ref[0]
    step = step_ref[0]
    row_blocks = rows // 8

    def element_blocks(view, modulus, mask):
        def corner_views(field, a):
            flat = [view(field, a, b) for b in (0, 1)]
            return [[x, pltpu.roll(x, nz - 1, 1)] for x in flat]

        speed = [[corner_views(3 + m, a) for a in (0, 1)] for m in range(3)]
        rate = None
        for m in range(3):
            for a in (0, 1):
                for b in (0, 1):
                    for c in (0, 1):
                        term = speed[m][a][b][c]
                        sign = (a, b, c)[m]
                        if rate is None:
                            rate = -term
                        else:
                            rate = rate + term if sign else rate - term
        bulk = (viscosity * mask) * jnp.maximum(-0.25 * rate, 0.0)
        factor = mask * modulus
        entries = []
        for m in range(3):
            for a in (0, 1):
                disps = corner_views(m, a)
                for b in (0, 1):
                    for c in (0, 1):
                        entries.append(factor * disps[b][c] + bulk * speed[m][a][b][c])
        return [
            jnp.concatenate([x[8 * t : 8 * t + 8, :] for x in entries], axis=0).astype(BF16)
            for t in range(entries[0].shape[0] // 8)
        ]

    def mapped(map_ref, blocks):
        wide = jnp.dot(map_ref[...], jnp.concatenate(blocks, axis=1), preferred_element_type=F32)
        return [wide[:, t * nz : (t + 1) * nz] for t in range(len(blocks))]

    inside_yz = ((iota((rows, nz), 0) <= rows - 2) & (iota((rows, nz), 1) <= nz - 2)).astype(F32)

    def element_plane(e, mask):
        blocks = element_blocks(lambda f, a, b: w[f, e + a, b : b + rows, :], w[6, e, 0:rows, :], mask)
        force = mapped(same_ref, blocks)
        carried = mapped(carry_ref, blocks[:-1]) if row_blocks > 1 else []
        return [force[0]] + [x + y for x, y in zip(force[1:], carried)]

    def part_of(force, m, a, c):
        at = ((m * 2 + a) * 2 + c) * 8
        return force[at : at + 8, :]

    def node_plane(e, force):
        for m in range(3):
            for t in range(row_blocks):
                part = [part_of(force[t], m, 0, c) + prev[m * 2 + c, t] for c in (0, 1)]
                internal = part[0] + pltpu.roll(part[1], 1, 1)
                at = slice(8 * t, 8 * t + 8)
                nv_ref[m, e - 1, at, :] = w[3 + m, e, at, :] - step * internal

    def advance(e):
        force = element_plane(e, inside_yz)
        node_plane(e, force)
        for m in range(3):
            for c in (0, 1):
                for t in range(row_blocks):
                    prev[m * 2 + c, t] = part_of(force[t], m, 1, c)

    prev[...] = jnp.zeros(prev.shape, F32)
    group = UNROLL if (planes - 1) % UNROLL == 0 else 1

    def advance_group(g):
        for i in range(group):
            advance(1 + g * group + i)

    @pl.loop(0, (planes - 1) // group)
    def _(g):
        advance_group(g)

    for m in range(3):
        for t in range(row_blocks):
            internal = prev[m * 2, t] + pltpu.roll(prev[m * 2 + 1, t], 1, 1)
            at = slice(8 * t, 8 * t + 8)
            nv_ref[m, planes - 1, at, :] = w[3 + m, planes, at, :] - step * internal

    lane_rows = iota((BLK, BLK), 0)

    def one_hot(lane):
        return jnp.concatenate(
            [(lane_rows == lane[r : r + 1, :]).astype(F32).astype(BF16) for r in range(lane.shape[0])], axis=1
        )

    own_valid = msg[3] >= 0.0
    own_wanted = jnp.where(own_valid, msg[3].astype(jnp.int32), 0)
    slot = (s + sub_count - own_wanted // (seg_blocks * BLK)) % sub_count
    own_block = slot * seg_blocks + own_wanted % (seg_blocks * BLK) // BLK
    own_block = jnp.where(own_valid, own_block, -1)
    own_hot = one_hot(own_wanted % BLK)
    own_rows = iota((sub_count * seg_blocks, BLK), 0)
    own_in_block = [own_rows == own_block[r : r + 1, :] for r in range(node_blocks)]
    own_parts = jnp.concatenate(split3(table[...]), axis=0)

    waits["nodes"].wait()

    group_rows = node_blocks * sub_count
    def contact(slots, parts, store, hot, in_block, valid, place):
        found = jnp.dot(parts, hot, preferred_element_type=F32)
        count = slots * 4 * seg_blocks
        found = found[0:count] + found[count : 2 * count] + found[2 * count : 3 * count]
        for f in range(4):
            for r in range(len(in_block)):
                picked = None
                for k in range(slots):
                    at = (k * 4 + f) * seg_blocks
                    field = found[at : at + seg_blocks, r * BLK : (r + 1) * BLK]
                    term = jnp.where(in_block[r][k * seg_blocks : (k + 1) * seg_blocks], field, 0.0)
                    picked = term if picked is None else picked + term
                store[f, r : r + 1, :] = jnp.sum(picked, axis=0, keepdims=True)
        tilt_x, tilt_y = store[0], store[1]
        unit = 1.0 / jnp.sqrt(1.0 + tilt_x * tilt_x + tilt_y * tilt_y)
        normal = (tilt_x * unit, tilt_y * unit, unit)
        depth = normal[0] * place[0] + normal[1] * place[1] + normal[2] * place[2] - store[2]
        pressure = jnp.where(valid, store[3] * jnp.maximum(depth, 0.0), 0.0)
        return [pressure * n for n in normal]

    wanted = nodes[3].astype(jnp.int32) - s * (seg_blocks * BLK)
    valid = (nodes[3] >= 0.0) & (wanted >= 0) & (wanted < seg_blocks * BLK)
    wanted = jnp.where(valid, wanted, 0)
    block = jnp.where(valid, wanted // BLK, -1)
    hot = one_hot(wanted % BLK)
    block_rows = iota((seg_blocks, BLK), 0)
    in_block = [block_rows == block[r : r + 1, :] for r in range(group_rows)]
    loads = contact(1, own_parts, values, hot, in_block, valid, nodes)
    spread = jnp.concatenate(
        [
            jnp.concatenate([jnp.where(in_block[r], loads[c][r : r + 1, :], 0.0) for r in range(group_rows)], axis=1)
            for c in range(3)
        ],
        axis=0,
    )
    high = spread.astype(BF16)
    low = (spread - high.astype(F32)).astype(BF16)
    summed = lax.dot_general(
        jnp.concatenate([high, low], axis=0), hot, (((1,), (1,)), ((), ())), preferred_element_type=F32
    )
    summed = summed[0 : 3 * seg_blocks] + summed[3 * seg_blocks :]
    for c in range(3):
        for b in range(seg_blocks):
            at = c * seg_blocks + b
            react_ref[c : c + 1, b * BLK : (b + 1) * BLK] = summed[at : at + 1, :]

    waits["tables"].wait()
    waits["rows"].wait()
    halo_wait(halo_recv, -1, (0,))
    parts = jnp.concatenate(split3(tables[...].reshape(sub_count * 4 * seg_blocks, BLK)), axis=0)
    loads = contact(sub_count, parts, own_values, own_hot, own_in_block, own_valid, msg)
    top = iota((nz, BLK), 0) == nz - 1
    for c in range(3):
        total = step * loads[c]
        for k in range(node_blocks):
            column = jnp.transpose(jnp.where(top, total[k : k + 1, :], 0.0)).reshape(block_planes, rows, nz)
            at = slice(k * block_planes, (k + 1) * block_planes)
            nv_ref[c, at, :, :] = nv_ref[c, at, :, :] - column

    sides = ((0, 0, s > 0), (1, rows - 1, s < sub_count - 1))
    along = iota((planes, nz), 0)
    inside_xz = ((along >= 1) & (iota((planes, nz), 1) <= nz - 2)).astype(F32)
    for k, y, present in sides:
        blocks = element_blocks(
            lambda f, a, b: xr[2 * k + b, f, a : a + planes, :],
            xr[2 * k, 6, 0:planes, :],
            inside_xz * present.astype(F32),
        )
        here = mapped(edge_ref.at[2 * k], blocks)
        after = mapped(edge_ref.at[2 * k + 1], blocks[1:]) if planes > 8 else []
        for t in range(planes // 8):
            force = here[t] + after[t] if t < len(after) else here[t]
            for m in range(3):
                at = m * 16
                internal = step * (force[at : at + 8, :] + pltpu.roll(force[at + 8 : at + 16, :], 1, 1))
                for j in range(8):
                    x = 8 * t + j
                    nv_ref[m, x, y : y + 1, :] = nv_ref[m, x, y : y + 1, :] - internal[j : j + 1, :]

    halo_wait(halo_recv, -1, (-1, 1))
    for k, y in ((1, 0), (2, rows - 1)):
        for edge, at in ((0, 0), (planes + 1, 3)):
            xc[k, :, at, :] = w[:, edge, y, :]
    for k in range(4):
        for edge, at in ((1, 1), (planes, 2)):
            xc[k, :, at, :] = xr[k, :, edge, :]

    lower = (d > 0).astype(F32)
    upper = (d < dom_count - 1).astype(F32)
    ahead = element_plane(planes, inside_yz * upper)
    behind = element_plane(0, inside_yz * lower)
    pair = iota((8, nz), 0)
    ends = jnp.where(pair == 0, lower, 0.0) + jnp.where(pair == 2, upper, 0.0)
    ends = jnp.where(iota((8, nz), 1) <= nz - 2, ends, 0.0)
    corners = [
        mapped(
            edge_ref.at[2 * k],
            element_blocks(
                lambda f, a, b: xc[2 * k + b, f, a : a + 8, :], xc[2 * k, 6, 0:8, :], ends * present.astype(F32)
            ),
        )[0]
        for k, y, present in sides
    ]
    for force, a, x in ((ahead, 0, planes - 1), (behind, 1, 0)):
        for m in range(3):
            for t in range(row_blocks):
                internal = part_of(force[t], m, a, 0) + pltpu.roll(part_of(force[t], m, a, 1), 1, 1)
                at = slice(8 * t, 8 * t + 8)
                nv_ref[m, x, at, :] = nv_ref[m, x, at, :] - step * internal
    for (k, y, present), force in zip(sides, corners):
        for m in range(3):
            at = m * 16
            internal = step * (force[at : at + 8, :] + pltpu.roll(force[at + 8 : at + 16, :], 1, 1))
            for j, x in ((0, 0), (1, planes - 1)):
                nv_ref[m, x, y : y + 1, :] = nv_ref[m, x, y : y + 1, :] - internal[j : j + 1, :]

    waits["nodes_sent"].wait()
    waits["tables_sent"].wait()
    halo_wait(halo_send, 1, (-1, 0, 1))


def store_kernel(nv_ref, react_ref, nv_out, react_out, sem):
    copies = [
        pltpu.make_async_copy(a, b, sem.at[i]) for i, (a, b) in enumerate(((nv_ref, nv_out), (react_ref, react_out)))
    ]
    for copy in copies:
        copy.start()
    for copy in copies:
        copy.wait()


def local(
    dom_count, sub_count, displacement, velocity, modulus, element_stiffness, viscosity, step_size, seg_tilt,
    seg_offset, seg_stiffness, projection, contact_flag, candidates,
):
    _, planes, rows, nz = displacement.shape
    seg_local = seg_offset.shape[0]
    seg_blocks = seg_local // BLK
    node_blocks = projection.shape[0]
    group_rows = node_blocks * sub_count
    vmem = pl.BlockSpec(memory_space=pltpu.VMEM)
    hbm = pl.BlockSpec(memory_space=pl.ANY)
    dma = pltpu.SemaphoreType.DMA
    results = pl.pallas_call(
        functools.partial(kernel, dom_count, sub_count),
        out_shape=(
            pltpu.VMEM(velocity.shape, F32),
            pltpu.VMEM((3, seg_local), F32),
        ),
        in_specs=[hbm] * 12,
        out_specs=(vmem, vmem),
        scratch_shapes=[
            pltpu.SMEM((1,), F32),
            pltpu.SMEM((1,), F32),
            pltpu.VMEM(candidates.shape, jnp.int32),
            pltpu.VMEM(element_stiffness.shape, BF16),
            pltpu.VMEM(seg_tilt.shape, F32),
            pltpu.VMEM(projection.shape, jnp.int32),
            pltpu.VMEM(contact_flag.shape, jnp.int32),
            pltpu.VMEM((7, planes + 2, rows + 8, nz), F32),
            pltpu.VMEM((4, 7, planes + 16, nz), F32),
            pltpu.VMEM((4, 7, 16, nz), F32),
            pltpu.VMEM((4, node_blocks, BLK), F32),
            pltpu.VMEM((4, group_rows, BLK), F32),
            pltpu.VMEM((sub_count, 4 * seg_blocks, BLK), F32),
            pltpu.VMEM((4, group_rows, BLK), F32),
            pltpu.VMEM((4, node_blocks, BLK), F32),
            pltpu.VMEM((96, 192), BF16),
            pltpu.VMEM((96, 192), BF16),
            pltpu.VMEM((4, 48, 192), BF16),
            pltpu.VMEM((6, rows // 8, 8, nz), F32),
            dma((11,)),
            dma((3,)),
            dma((3,)),
            dma((4,)),
        ],
        compiler_params=pltpu.CompilerParams(collective_id=0, has_side_effects=True),
    )(
        viscosity.reshape(1),
        step_size.reshape(1),
        candidates,
        element_stiffness,
        seg_tilt,
        seg_offset.reshape(seg_blocks, BLK),
        seg_stiffness.reshape(seg_blocks, BLK),
        projection,
        contact_flag,
        displacement,
        velocity,
        modulus,
    )
    return pl.pallas_call(
        store_kernel,
        out_shape=tuple(jax.ShapeDtypeStruct(x.shape, F32) for x in results),
        in_specs=[vmem, vmem],
        out_specs=(hbm, hbm),
        scratch_shapes=[dma((2,))],
    )(*(pltpu.with_memory_space_constraint(x, pltpu.VMEM) for x in results))


def solution(mesh):
    return jax.shard_map(
        functools.partial(local, mesh.shape["dom"], mesh.shape["sub"]),
        mesh=mesh,
        in_specs=(
            P(None, "dom", "sub", None),
            P(None, "dom", "sub", None),
            P("dom", "sub", None),
            P(),
            P(),
            P(),
            P(None, ("dom", "sub")),
            P(("dom", "sub")),
            P(("dom", "sub")),
            P(("dom", "sub"), None),
            P(("dom", "sub"), None),
            P(("dom", "sub"), None),
        ),
        out_specs=(P(None, "dom", "sub", None), P(None, ("dom", "sub"))),
        check_vma=False,
    )
```
